512 devices in a mesh: row: 16 (over x, z_hi), col: 32 (over z_lo, y, core).
Axes of the slice: x: 4, y: 8, z: 8 (z_hi: 4, z_lo: 2; z = z_hi * 2 + z_lo), core: 2. Of those that a mesh axis runs over, the one named last changes fastest.
Arguments:
- inputs: bfloat16 [512, 1792, 128], P('row', 'col'), may hold values from -6 to 6
- cotangent: bfloat16 [512, 1792, 128], P('row', 'col'), may hold values from -6 to 6
- w_conv: bfloat16 [3, 3, 128, 128], replicated, may hold values from -0.1875 to 0.1875
- w_down: bfloat16 [3, 3, 128, 256], replicated, may hold values from -0.1875 to 0.1875
- w_up: bfloat16 [2, 2, 256, 128], replicated, may hold values from -0.375 to 0.375
Outputs:
- output: bfloat16 [512, 1792, 128], P('row', 'col')
- grad_inputs: bfloat16 [512, 1792, 128], P('row', 'col')
- grad_conv: float32 [147456], P(('row', 'col'))
- grad_down: float32 [294912], P(('row', 'col'))
- grad_up: float32 [131072], P(('row', 'col'))
The draws below stay inside these ranges and needn't reach their ends.
All inputs are finite; a program needn't handle non-finite values.
Results may differ from the reference program's by a relative error of at most 0.013.
Values may be sent and summed in bfloat16 or wider, within the bound.
No kernel may reach another device: no remote copies, remote signals or barrier semaphores. Data moves between devices by JAX's collectives and lax.ppermute only.
A program may use at most 64 MiB of HBM per device.

```python
import jax
import jax.numpy as jnp
from jax import lax

C1 = 128
C2 = 256
NH = 512
NW = 1792


def block_levels(own_key, shape, shards, least, largest):
    level = 1.0
    for axis_at, shards_of in shards:
        heights = jax.random.uniform(jax.random.fold_in(jax.random.fold_in(own_key, 6), axis_at), (shards_of,), jnp.float32, least / len(shards), largest / len(shards))
        level = level * jnp.repeat(jnp.exp(heights), shape[axis_at] // shards_of).reshape((-1,) + (1,) * (len(shape) - 1 - axis_at))
    return level


def noise(stream_key, dims, spread, most, split=(), held_as=jnp.bfloat16):
    drawn = jax.random.normal(stream_key, dims, jnp.float32) * spread
    if len(split) > 0:
        drawn = block_levels(stream_key, dims, split, -0.22, 0.18) * drawn
    return jnp.clip(drawn, min=-most, max=most).astype(held_as)


def setup_inputs(seed: int = 0) -> dict:
    key_list = jax.random.split(jax.random.key(seed), 6)
    return {
        "inputs": noise(key_list[0], (NH, NW, C1), 1.0, 6.0, ((0, 16), (1, 32))),
        "cotangent": noise(key_list[1], (NH, NW, C1), 1.0, 6.0, ((0, 16), (1, 32))),
        "w_conv": noise(key_list[2], (3, 3, C1, C1), (9 * C1) ** -0.5, 0.1875),
        "w_down": noise(key_list[3], (3, 3, C1, C2), (9 * C1) ** -0.5, 0.1875),
        "w_up": noise(key_list[4], (2, 2, C2, C1), C2 ** -0.5, 0.375),
    }


def conv_same(field, kernel):
    return lax.conv_general_dilated(field[None], kernel, (1, 1), ((1, 1), (1, 1)), dimension_numbers=('NHWC', 'HWIO', 'NHWC'), precision=lax.Precision.HIGHEST)[0]

def conv_down(field, kernel):
    return lax.conv_general_dilated(field[None], kernel, (2, 2), ((1, 1), (1, 1)), dimension_numbers=('NHWC', 'HWIO', 'NHWC'), precision=lax.Precision.HIGHEST)[0]

def silu_slope(value):
    sig = jax.nn.sigmoid(value)
    return sig * (1.0 + value * (1.0 - sig))

def forward_fine(inputs, w_conv):
    pre = conv_same(inputs.astype(jnp.float32), w_conv.astype(jnp.float32))
    return (pre, jax.nn.silu(pre).astype(jnp.bfloat16))

def reference(inputs, cotangent, w_conv, w_down, w_up):
    pre, fine = forward_fine(inputs, w_conv)
    coarse_pre = conv_down(fine.astype(jnp.float32), w_down.astype(jnp.float32))
    coarse = jax.nn.silu(coarse_pre).astype(jnp.bfloat16)
    up_f = w_up.astype(jnp.float32)
    upsampled = jnp.einsum('mnc,pqco->mpnqo', coarse.astype(jnp.float32), up_f, precision=lax.Precision.HIGHEST).reshape(NH, NW, C1)
    output = (fine.astype(jnp.float32) + upsampled).astype(jnp.bfloat16)
    upsampled = None
    cot_r = cotangent.astype(jnp.float32).reshape(NH // 2, 2, NW // 2, 2, C1)
    grad_coarse = jnp.einsum('mpnqo,pqco->mnc', cot_r, up_f, precision=lax.Precision.HIGHEST)
    up_sum = jnp.einsum('mnc,mpnqo->pqco', coarse.astype(jnp.float32), cot_r, precision=lax.Precision.HIGHEST)
    cot_r = None
    grad_cpre = (grad_coarse * silu_slope(coarse_pre)).astype(jnp.bfloat16)
    _, back_down = jax.vjp(conv_down, fine.astype(jnp.float32), w_down.astype(jnp.float32))
    down_in, down_sum = back_down(grad_cpre.astype(jnp.float32))
    grad_fine = cotangent.astype(jnp.float32) + down_in
    down_in = None
    grad_pre = (grad_fine * silu_slope(pre)).astype(jnp.bfloat16)
    grad_fine = None
    pre = None
    _, back_conv = jax.vjp(conv_same, inputs.astype(jnp.float32), w_conv.astype(jnp.float32))
    grad_x, conv_sum = back_conv(grad_pre.astype(jnp.float32))
    grad_inputs = grad_x.astype(jnp.bfloat16)
    scale = 1.0 / jnp.sqrt(jnp.float32(NH * NW))
    return (output, grad_inputs, (conv_sum * scale).reshape(-1), (down_sum * scale).reshape(-1), (up_sum * scale).reshape(-1))
```

```python
import functools
import math

import jax
import jax.numpy as jnp
from jax import lax
from jax.experimental import pallas as pl
from jax.experimental.pallas import tpu as pltpu
from jax.sharding import PartitionSpec as P

BF = jnp.bfloat16
F32 = jnp.float32
NN = (((1,), (0,)), ((), ()))
NT = (((1,), (1,)), ((), ()))
TN = (((0,), (0,)), ((), ()))
LANES = 32


def mm(left, right, dims):
    return lax.dot_general(left, right, dims, preferred_element_type=F32)


def sigmoid(value):
    return 1.0 / (1.0 + jnp.exp(-value))


def weights_kernel(wc, wd, wu, conv_fwd, conv_bwd, up, down_even, down_odd):
    zero = jnp.zeros((128, 128), BF)
    for p in range(3):
        for blk in range(4):
            rows = slice(blk * 128, (blk + 1) * 128)
            conv_fwd[p, rows, 0:128] = wc[p, blk] if blk < 3 else zero
            conv_fwd[p, rows, 128:256] = wc[p, blk - 1] if blk > 0 else zero
            conv_bwd[p, 0:128, rows] = wc[p, 2 - blk] if blk < 3 else zero
            conv_bwd[p, 128:256, rows] = wc[p, 3 - blk] if blk > 0 else zero
    for p in range(2):
        for q in range(2):
            up[:, (2 * p + q) * 128 : (2 * p + q + 1) * 128] = wu[p, q]
    wide = jnp.zeros((128, 256), BF)
    down_even[0:128, 0:256] = wd[1, 1]
    down_even[0:128, 256:512] = wide
    down_even[128:256, 0:256] = wd[1, 2]
    down_even[128:256, 256:512] = wd[1, 0]
    down_odd[0:128, 0:256] = wd[2, 1]
    down_odd[0:128, 256:512] = wide
    down_odd[0:128, 512:768] = wd[0, 1]
    down_odd[0:128, 768:1024] = wide
    down_odd[128:256, 0:256] = wd[2, 2]
    down_odd[128:256, 256:512] = wd[2, 0]
    down_odd[128:256, 512:768] = wd[0, 2]
    down_odd[128:256, 768:1024] = wd[0, 0]


def prepare_weights(w_conv, w_down, w_up):
    shapes = ((3, 512, 256), (3, 256, 512), (256, 512), (256, 512), (256, 1024))
    return pl.pallas_call(
        weights_kernel,
        out_shape=tuple(jax.ShapeDtypeStruct(s, BF) for s in shapes),
        name="weights",
    )(w_conv, w_down, w_up)


CONV_ROWS = ((0, 1, 2), (2, 3, 4), (4, 5, 6), (6, 7, 8))
DOWN_ROWS = ((0, 1, 2, 3, 4), (4, 5, 6, 7, 8), (9, 10, 11, 12, 13), (13, 14, 15, 16, 17))
UP_ROWS = ((0, 1), (2, 3), (4, 5), (6, 7))


def pack(core, ref, conv_acc, down_acc, up_acc):
    k = 0
    for owner in (core, core + 2):
        for row in CONV_ROWS[owner]:
            value = conv_acc[pl.ds(row, 128, stride=9), :]
            ref[:, 32 * k : 32 * k + 32, :] = value.reshape(4, 32, 128).astype(BF)
            k += 1
        for row in DOWN_ROWS[owner]:
            value = down_acc[row % 2, pl.ds(row // 2, 128, stride=9), :]
            ref[:, 32 * k : 32 * k + 32, :] = value.reshape(4, 32, 128).astype(BF)
            k += 1
        for row in UP_ROWS[owner]:
            value = up_acc[pl.ds(row, 128, stride=8), :]
            ref[:, 32 * k : 32 * k + 32, :] = value.reshape(4, 32, 128).astype(BF)
            k += 1


def level_kernel(
    edge, x, c, top, bot, left, right, w_fwd, w_bwd, w_down, w_up, w_even, w_odd,
    out, gx, keep, send,
    conv_acc, down_acc, up_acc, xs, cs, x4, c4, f3, slope, gs, coarse_own, g_own, g4, pre_own, mix,
):
    for ref in (xs, cs):
        ref[:, 0:8, :] = jnp.zeros((ref.shape[0], 8, 128), F32)
        ref[:, 64:72, :] = jnp.zeros((ref.shape[0], 8, 128), F32)
    xs[4:36, 8:64, :] = x[...].astype(F32)
    xs[0:4, 8:64, :] = top[0:4].astype(F32)
    xs[36:39, 8:64, :] = bot[0:3].astype(F32)
    xs[0:39, 4:8, :] = left[0:39].astype(F32)
    xs[0:39, 64:68, :] = right[0:39].astype(F32)
    cs[2:34, 8:64, :] = c[...].astype(F32)
    cs[0:2, 8:64, :] = top[4:6].astype(F32)
    cs[34:36, 8:64, :] = bot[3:5].astype(F32)
    cs[0:36, 4:8, :] = left[39:75].astype(F32)
    cs[0:36, 64:68, :] = right[39:75].astype(F32)
    for r in range(39):
        for k in range(4):
            x4[r, :, k * 128 : (k + 1) * 128] = xs[r, pl.ds(3 + k, 32, stride=2), :].astype(BF)
    x4[39] = jnp.zeros((32, 512), BF)
    for ai in range(18):
        for p in range(2):
            for q in range(2):
                k = 2 * p + q
                c4[ai, :, k * 128 : (k + 1) * 128] = cs[
                    2 * ai + p, pl.ds(4 + q, 32, stride=2), :
                ].astype(BF)

    is_top, is_bot = edge[0] > 0, edge[1] > 0
    is_left, is_right = edge[2] > 0, edge[3] > 0
    half = lax.broadcasted_iota(jnp.int32, (32, 256), 0) - 2
    in_grid = ((half >= 0) | jnp.logical_not(is_left)) & ((half < 28) | jnp.logical_not(is_right))
    in_grid = jnp.where(in_grid, 1.0, 0.0)
    own = jnp.where((half >= 0) & (half < 28), 1.0, 0.0)
    keep_top = jnp.where(is_top, 0.0, 1.0)
    keep_bot = jnp.where(is_bot, 0.0, 1.0)

    for first, count in ((0, 8), (8, 8), (16, 8), (24, 8), (32, 6)):
        pre = None
        for p in range(3):
            window = x4[first + p : first + p + count].reshape(count * 32, 512)
            term = mm(window, w_fwd[p], NN)
            pre = term if pre is None else pre + term
        sig = sigmoid(pre)
        slope[first : first + count] = (sig * (1.0 + pre * (1.0 - sig))).reshape(count, 32, 256)
        fine = ((pre * sig).reshape(count, 32, 256) * in_grid[None]).reshape(count * 32, 256)
        if first == 0 or first == 32:
            row = lax.broadcasted_iota(jnp.int32, (count * 32, 256), 0) // 32
            if first == 0:
                fine = jnp.where(row < 3, fine * keep_top, fine)
            else:
                fine = jnp.where(row >= 3, fine * keep_bot, fine)
        rounded = fine.astype(BF).reshape(count, 32, 256)
        behind = pltpu.roll(fine[:, 128:256], 1, 0).astype(BF).reshape(count, 32, 128)
        f3[first : first + count, :, 0:128] = behind
        f3[first : first + count, :, 128:384] = rounded

    for first, count in ((0, 9), (9, 9)):
        parts = []
        for p in range(3):
            parts.append(
                jnp.concatenate([f3[2 * ai + p] for ai in range(first, first + count)], axis=0)
            )
        cpre = mm(jnp.concatenate(parts, axis=1), w_down[...], NN)
        sig = sigmoid(cpre)
        coarse = cpre * sig
        slope_c = sig * (1.0 + cpre * (1.0 - sig))
        grad_coarse = mm(c4[first : first + count].reshape(count * 32, 512), w_up[...], NT)
        grad = grad_coarse * slope_c
        ahead = pltpu.roll(grad, count * 32 - 1, 0)
        gs[first : first + count, :, 0:256] = grad.astype(BF).reshape(count, 32, 256)
        gs[first : first + count, :, 256:512] = ahead.astype(BF).reshape(count, 32, 256)
        low, high = max(first, 1), min(first + count, 17)
        inner = slice((low - first) * 32, (high - first) * 32)
        coarse_own[low - 1 : high - 1] = (
            (coarse[inner].reshape(high - low, 32, 256) * own[None]).astype(BF)
        )
        g_own[low - 1 : high - 1] = (
            (grad[inner].reshape(high - low, 32, 256) * own[None]).astype(BF)
        )

    for first in (0, 8):
        up = mm(coarse_own[first : first + 8].reshape(256, 256), w_up[...], NN)
        for a in range(first, first + 8):
            for p in range(2):
                for q in range(2):
                    k = 2 * p + q
                    value = up[(a - first) * 32 : (a - first + 1) * 32, k * 128 : (k + 1) * 128]
                    value = value + f3[2 * a + p + 3, :, 128 + q * 128 : 256 + q * 128].astype(F32)
                    mix[2 * a + p, pl.ds(4 + q, 32, stride=2), :] = value
    out[...] = mix[:, 8:64, :].astype(BF)
    coarse_flat = coarse_own[...].reshape(512, 256)
    res = mm(coarse_flat, c4[1:17].reshape(512, 512), TN)
    for k in range(4):
        up_acc[k * 256 : (k + 1) * 256, :] = res[:, k * 128 : (k + 1) * 128]
    g_flat = g_own[...].reshape(512, 256)
    for p in range(3):
        window = jnp.concatenate([f3[2 * a + p + 2] for a in range(16)], axis=0)
        res = mm(window, g_flat, TN)
        for side in range(2):
            down_acc[side, p * 384 : (p + 1) * 384, :] = res[:, side * 128 : (side + 1) * 128]

    for first, count in ((0, 9), (9, 8)):
        for odd in (True, False):
            here = gs[first : first + count].reshape(count * 32, 512)
            below = gs[first + 1 : first + 1 + count].reshape(count * 32, 512)
            if odd:
                spread = mm(jnp.concatenate([here, below], axis=1), w_odd[...], NT)
                cot = c4[first : first + count, :, 256:512].reshape(count * 32, 256)
                at = 2
            else:
                spread = mm(below, w_even[...], NT)
                cot = c4[first + 1 : first + 1 + count, :, 0:256].reshape(count * 32, 256)
                at = 3
            slopes = jnp.concatenate([slope[2 * ai + at] for ai in range(first, first + count)], 0)
            grad = (cot.astype(F32) + spread) * slopes
            grad = (grad.reshape(count, 32, 256) * in_grid[None]).reshape(count * 32, 256)
            if first == 0 and odd:
                row = lax.broadcasted_iota(jnp.int32, (count * 32, 256), 0)
                grad = jnp.where(row < 32, grad * keep_top, grad)
            if first != 0 and not odd:
                row = lax.broadcasted_iota(jnp.int32, (count * 32, 256), 0)
                grad = jnp.where(row >= (count - 1) * 32, grad * keep_bot, grad)
            behind = pltpu.roll(grad[:, 128:256], 1, 0).astype(BF)
            ahead = pltpu.roll(grad[:, 0:128], count * 32 - 1, 0).astype(BF)
            rounded = grad.astype(BF)
            kept = (grad.reshape(count, 32, 256) * own[None]).astype(BF)
            for ai in range(first, first + count):
                g_row = 2 * ai + (0 if odd else 1)
                rows = slice((ai - first) * 32, (ai - first + 1) * 32)
                g4[g_row, :, 0:128] = behind[rows]
                g4[g_row, :, 128:384] = rounded[rows]
                g4[g_row, :, 384:512] = ahead[rows]
                if 1 <= g_row <= 32:
                    pre_own[g_row - 1] = kept[ai - first]

    for first in (0, 8, 16, 24):
        total = None
        for p in range(3):
            window = g4[first + 2 - p : first + 10 - p].reshape(256, 512)
            term = mm(window, w_bwd[p], NT)
            total = term if total is None else total + term
        for i in range(first, first + 8):
            for q in range(2):
                mix[i, pl.ds(4 + q, 32, stride=2), :] = total[
                    (i - first) * 32 : (i - first + 1) * 32, q * 128 : (q + 1) * 128
                ]
    gx[...] = mix[:, 8:64, :].astype(BF)
    flat = pre_own[...].reshape(1024, 256)
    for p in range(3):
        res = mm(flat, x4[p + 3 : p + 35].reshape(1024, 512), TN)
        for q in range(3):
            tap = res[0:128, q * 128 : (q + 1) * 128] + res[128:256, (q + 1) * 128 : (q + 2) * 128]
            conv_acc[(3 * p + q) * 128 : (3 * p + q + 1) * 128, :] = tap.T

    @pl.when(edge[4] == 0)
    def _():
        pack(0, keep, conv_acc, down_acc, up_acc)
        pack(1, send, conv_acc, down_acc, up_acc)

    @pl.when(edge[4] != 0)
    def _():
        pack(1, keep, conv_acc, down_acc, up_acc)
        pack(0, send, conv_acc, down_acc, up_acc)


def level(edge, x, c, top, bot, left, right, weights, w_down):
    w_fwd, w_bwd, w_up, w_even, w_odd = weights
    vmem = pl.BlockSpec(memory_space=pltpu.VMEM)
    return pl.pallas_call(
        level_kernel,
        out_shape=(
            jax.ShapeDtypeStruct((32, 56, 128), BF),
            jax.ShapeDtypeStruct((32, 56, 128), BF),
            jax.ShapeDtypeStruct((4, 640, 128), BF),
            jax.ShapeDtypeStruct((4, 640, 128), BF),
        ),
        in_specs=[pl.BlockSpec(memory_space=pltpu.SMEM)] + [vmem] * 12,
        out_specs=(vmem,) * 4,
        scratch_shapes=[
            pltpu.VMEM((1160, 128), F32),
            pltpu.VMEM((2, 1160, 128), F32),
            pltpu.VMEM((1032, 128), F32),
            pltpu.VMEM((39, 72, 128), F32),
            pltpu.VMEM((36, 72, 128), F32),
            pltpu.VMEM((40, 32, 512), BF),
            pltpu.VMEM((18, 32, 512), BF),
            pltpu.VMEM((38, 32, 384), BF),
            pltpu.VMEM((38, 32, 256), F32),
            pltpu.VMEM((18, 32, 512), BF),
            pltpu.VMEM((16, 32, 256), BF),
            pltpu.VMEM((16, 32, 256), BF),
            pltpu.VMEM((34, 32, 512), BF),
            pltpu.VMEM((32, 32, 256), BF),
            pltpu.VMEM((32, 72, 128), F32),
        ],
        compiler_params=pltpu.CompilerParams(vmem_limit_bytes=56 * 1024 * 1024),
        name="level",
    )(edge, x, c, top, bot, left, right, w_fwd, w_bwd, w_down, w_up, w_even, w_odd)


def chain(axis, step):
    count = lax.axis_size(axis)
    return [(i, i + step) for i in range(count) if 0 <= i + step < count]


def rows_kernel(x_last, x_first, c_last, c_first, down, up):
    down[0:4] = x_last[...]
    down[4:6] = c_last[...]
    up[0:3] = x_first[0:3]
    up[3:5] = c_first[...]


def cols_kernel(
    x_last, x_first, c_last, c_first, top_last, top_first, bot_last, bot_first, right, left
):
    for out, cols, x, c, top, bot in (
        (right, slice(4, 8), x_last, c_last, top_last, bot_last),
        (left, slice(0, 4), x_first, c_first, top_first, bot_first),
    ):
        out[0:4] = top[0:4, cols, :]
        out[4:36] = x[:, cols, :]
        out[36:39] = bot[0:3, cols, :]
        out[39:41] = top[4:6, cols, :]
        out[41:73] = c[:, cols, :]
        out[73:75] = bot[3:5, cols, :]


def row_block(count, at):
    return pl.BlockSpec((count, 56, 128), lambda i: (at, 0, 0))


def col_block(count, at):
    return pl.BlockSpec((count, 8, 128), lambda i: (0, at, 0))


def exchange(x, c):
    down, up = pl.pallas_call(
        rows_kernel,
        grid=(1,),
        out_shape=(
            jax.ShapeDtypeStruct((6, 56, 128), BF),
            jax.ShapeDtypeStruct((5, 56, 128), BF),
        ),
        in_specs=[row_block(4, 7), row_block(4, 0), row_block(2, 15), row_block(2, 0)],
        out_specs=(row_block(6, 0), row_block(5, 0)),
        name="rows",
    )(x, x, c, c)
    top = lax.ppermute(down, "row", chain("row", 1))
    bot = lax.ppermute(up, "row", chain("row", -1))
    whole = pl.BlockSpec((75, 4, 128), lambda i: (0, 0, 0))
    going_right, going_left = pl.pallas_call(
        cols_kernel,
        grid=(1,),
        out_shape=(jax.ShapeDtypeStruct((75, 4, 128), BF),) * 2,
        in_specs=[col_block(n, at) for n in (32, 32, 6, 5) for at in (6, 0)],
        out_specs=(whole, whole),
        name="cols",
    )(x, x, c, c, top, top, bot, bot)
    left = lax.ppermute(going_right, "col", chain("col", 1))
    right = lax.ppermute(going_left, "col", chain("col", -1))
    return top, bot, left, right


def local_terms(inputs, cotangent, w_conv, w_down, w_up):
    n_row, n_col = lax.axis_size("row"), lax.axis_size("col")
    at_row, at_col = lax.axis_index("row"), lax.axis_index("col")
    edge = jnp.stack(
        [at_row == 0, at_row == n_row - 1, at_col == 0, at_col == n_col - 1, at_col % 2 == 1]
    ).astype(jnp.int32)
    weights = prepare_weights(w_conv, w_down, w_up)
    halo = exchange(inputs, cotangent)
    return level(edge, inputs, cotangent, *halo, weights, w_down.reshape(1152, 256))


def spread_kernel(received, out, total):
    total[0:640, :] = jnp.sum(received[...].astype(F32), axis=0)
    for z in range(8):
        for y in range(8):
            first = (y % 2) * 320 + z * 4 + y // 2
            out[8 * z + y, 0:10, :] = total[pl.ds(first, 10, stride=32), :].astype(BF)


def finish_kernel(scale, at, received, conv, down, up):
    rows = jnp.sum(received[...].astype(F32), axis=0)[0:10] * scale
    for which in range(4):

        @pl.when(at[0] == which)
        def _():
            for ref, base, names, size in (
                (conv, 0, CONV_ROWS, 288), (down, 3, DOWN_ROWS, 576), (up, 8, UP_ROWS, 256)
            ):
                start = (base - names[which][0]) * 128 + which * size
                done = 0
                while done < size:
                    row, lane = divmod(start + done, 128)
                    count = min(128 - lane, size - done)
                    ref[0:1, done : done + count] = rows[row : row + 1, lane : lane + count]
                    done += count


def coordinates():
    def device(x, y, z, core):
        return (x * 4 + z // 2) * 32 + (z % 2) * 16 + y * 2 + core

    across = [
        [device(x, y, z, k) for x in range(4)]
        for z in range(8) for y in range(8) for k in range(2)
    ]
    plane = [
        [device(x, y, z, k) for z in range(8) for y in range(8)]
        for x in range(4) for k in range(2)
    ]
    return across, plane


def reduce_owners(keep, send, scale):
    mesh = ("row", "col")
    across, plane = coordinates()
    other = lax.ppermute(send, "col", [(i, i ^ 1) for i in range(32)])
    pair = (keep.astype(F32) + other.astype(F32)).astype(BF)
    got = lax.all_to_all(pair, mesh, 0, 0, axis_index_groups=across, tiled=True)
    spread = pl.pallas_call(
        spread_kernel,
        out_shape=jax.ShapeDtypeStruct((64, 16, 128), BF),
        scratch_shapes=[pltpu.VMEM((672, 128), F32)],
        name="spread",
    )(got)
    got = lax.all_to_all(spread, mesh, 0, 0, axis_index_groups=plane, tiled=True)
    at = (lax.axis_index("col") % 4).astype(jnp.int32).reshape(1)
    sums = pl.pallas_call(
        functools.partial(finish_kernel, scale),
        out_shape=tuple(jax.ShapeDtypeStruct((1, n), F32) for n in (288, 576, 256)),
        in_specs=[
            pl.BlockSpec(memory_space=pltpu.SMEM),
            pl.BlockSpec(memory_space=pltpu.VMEM),
        ],
        name="finish",
    )(at, got)
    return [part.reshape(-1) for part in sums]


def body(inputs, cotangent, w_conv, w_down, w_up):
    output, grad_inputs, keep, send = local_terms(inputs, cotangent, w_conv, w_down, w_up)
    rows, cols, _ = inputs.shape
    scale = 1.0 / math.sqrt(rows * lax.axis_size("row") * cols * lax.axis_size("col"))
    return (output, grad_inputs, *reduce_owners(keep, send, scale))


def solution(mesh):
    grid = P("row", "col", None)
    flat = P(("row", "col"))
    return jax.shard_map(
        body,
        mesh=mesh,
        in_specs=(grid, grid, P(), P(), P()),
        out_specs=(grid, grid, flat, flat, flat),
        check_vma=False,
    )
```

```python
import functools
import math

import jax
import jax.numpy as jnp
from jax import lax
from jax.experimental import pallas as pl
from jax.experimental.pallas import tpu as pltpu
from jax.sharding import PartitionSpec as P

BF = jnp.bfloat16
F32 = jnp.float32
NN = (((1,), (0,)), ((), ()))
NT = (((1,), (1,)), ((), ()))
TN = (((0,), (0,)), ((), ()))
LANES = 32


def held(shape, dtype=BF):
    return pltpu.VMEM(shape, dtype)


def far(*arrays):
    return tuple(pltpu.with_memory_space_constraint(a, pltpu.HBM) for a in arrays)


def pin(*arrays):
    return tuple(pltpu.with_memory_space_constraint(a, pltpu.VMEM) for a in arrays)


def mm(left, right, dims):
    return lax.dot_general(left, right, dims, preferred_element_type=F32)


def sigmoid(value):
    return 1.0 / (1.0 + jnp.exp(-value))


def weights_kernel(wc, wd, wu, conv_fwd, conv_bwd, up, down_even, down_odd):
    zero = jnp.zeros((128, 128), BF)
    for p in range(3):
        for blk in range(4):
            rows = slice(blk * 128, (blk + 1) * 128)
            conv_fwd[p, rows, 0:128] = wc[p, blk] if blk < 3 else zero
            conv_fwd[p, rows, 128:256] = wc[p, blk - 1] if blk > 0 else zero
            conv_bwd[p, 0:128, rows] = wc[p, 2 - blk] if blk < 3 else zero
            conv_bwd[p, 128:256, rows] = wc[p, 3 - blk] if blk > 0 else zero
    for p in range(2):
        for q in range(2):
            up[:, (2 * p + q) * 128 : (2 * p + q + 1) * 128] = wu[p, q]
    wide = jnp.zeros((128, 256), BF)
    down_even[0:128, 0:256] = wd[1, 1]
    down_even[0:128, 256:512] = wide
    down_even[128:256, 0:256] = wd[1, 2]
    down_even[128:256, 256:512] = wd[1, 0]
    down_odd[0:128, 0:256] = wd[2, 1]
    down_odd[0:128, 256:512] = wide
    down_odd[0:128, 512:768] = wd[0, 1]
    down_odd[0:128, 768:1024] = wide
    down_odd[128:256, 0:256] = wd[2, 2]
    down_odd[128:256, 256:512] = wd[2, 0]
    down_odd[128:256, 512:768] = wd[0, 2]
    down_odd[128:256, 768:1024] = wd[0, 0]


def prepare_weights(w_conv, w_down, w_up):
    shapes = ((3, 512, 256), (3, 256, 512), (256, 512), (256, 512), (256, 1024))
    return pl.pallas_call(
        weights_kernel,
        out_shape=tuple(jax.ShapeDtypeStruct(s, BF) for s in shapes),
        name="weights",
    )(w_conv, w_down, w_up)


CONV_ROWS = ((0, 1, 2), (2, 3, 4), (4, 5, 6), (6, 7, 8))
DOWN_ROWS = ((0, 1, 2, 3, 4), (4, 5, 6, 7, 8), (9, 10, 11, 12, 13), (13, 14, 15, 16, 17))
UP_ROWS = ((0, 1), (2, 3), (4, 5), (6, 7))


def pack(core, ref, conv_acc, down_acc, up_acc):
    k = 0
    for owner in (core, core + 2):
        for row in CONV_ROWS[owner]:
            value = conv_acc[pl.ds(row, 128, stride=9), :]
            ref[:, 32 * k : 32 * k + 32, :] = value.reshape(4, 32, 128).astype(BF)
            k += 1
        for row in DOWN_ROWS[owner]:
            value = down_acc[row % 2, pl.ds(row // 2, 128, stride=9), :]
            ref[:, 32 * k : 32 * k + 32, :] = value.reshape(4, 32, 128).astype(BF)
            k += 1
        for row in UP_ROWS[owner]:
            value = up_acc[pl.ds(row, 128, stride=8), :]
            ref[:, 32 * k : 32 * k + 32, :] = value.reshape(4, 32, 128).astype(BF)
            k += 1


def level_kernel(
    edge, x, c, top, bot, left, right, w_fwd, w_bwd, w_down, w_up, w_even, w_odd,
    out, gx, keep, send,
    conv_acc, down_acc, up_acc, xs, cs, x4, c4, f3, slope, gs, coarse_own, g_own, g4, pre_own, mix,
):
    for ref in (xs, cs):
        ref[:, 0:8, :] = jnp.zeros((ref.shape[0], 8, 128), F32)
        ref[:, 64:72, :] = jnp.zeros((ref.shape[0], 8, 128), F32)
    xs[4:36, 8:64, :] = x[...].astype(F32)
    xs[0:4, 8:64, :] = top[0:4].astype(F32)
    xs[36:39, 8:64, :] = bot[0:3].astype(F32)
    xs[0:39, 4:8, :] = left[0:39].astype(F32)
    xs[0:39, 64:68, :] = right[0:39].astype(F32)
    cs[2:34, 8:64, :] = c[...].astype(F32)
    cs[0:2, 8:64, :] = top[4:6].astype(F32)
    cs[34:36, 8:64, :] = bot[3:5].astype(F32)
    cs[0:36, 4:8, :] = left[39:75].astype(F32)
    cs[0:36, 64:68, :] = right[39:75].astype(F32)
    for r in range(39):
        for k in range(4):
            x4[r, :, k * 128 : (k + 1) * 128] = xs[r, pl.ds(3 + k, 32, stride=2), :].astype(BF)
    x4[39] = jnp.zeros((32, 512), BF)
    for ai in range(18):
        for p in range(2):
            for q in range(2):
                k = 2 * p + q
                c4[ai, :, k * 128 : (k + 1) * 128] = cs[
                    2 * ai + p, pl.ds(4 + q, 32, stride=2), :
                ].astype(BF)

    is_top, is_bot = edge[0] > 0, edge[1] > 0
    is_left, is_right = edge[2] > 0, edge[3] > 0
    half = lax.broadcasted_iota(jnp.int32, (32, 256), 0) - 2
    in_grid = ((half >= 0) | jnp.logical_not(is_left)) & ((half < 28) | jnp.logical_not(is_right))
    in_grid = jnp.where(in_grid, 1.0, 0.0)
    own = jnp.where((half >= 0) & (half < 28), 1.0, 0.0)
    keep_top = jnp.where(is_top, 0.0, 1.0)
    keep_bot = jnp.where(is_bot, 0.0, 1.0)

    for first, count in ((0, 8), (8, 8), (16, 8), (24, 8), (32, 6)):
        pre = None
        for p in range(3):
            window = x4[first + p : first + p + count].reshape(count * 32, 512)
            term = mm(window, w_fwd[p], NN)
            pre = term if pre is None else pre + term
        sig = sigmoid(pre)
        slope[first : first + count] = (sig * (1.0 + pre * (1.0 - sig))).reshape(count, 32, 256)
        fine = ((pre * sig).reshape(count, 32, 256) * in_grid[None]).reshape(count * 32, 256)
        if first == 0 or first == 32:
            row = lax.broadcasted_iota(jnp.int32, (count * 32, 256), 0) // 32
            if first == 0:
                fine = jnp.where(row < 3, fine * keep_top, fine)
            else:
                fine = jnp.where(row >= 3, fine * keep_bot, fine)
        rounded = fine.astype(BF).reshape(count, 32, 256)
        behind = pltpu.roll(fine[:, 128:256], 1, 0).astype(BF).reshape(count, 32, 128)
        f3[first : first + count, :, 0:128] = behind
        f3[first : first + count, :, 128:384] = rounded

    for first, count in ((0, 9), (9, 9)):
        parts = []
        for p in range(3):
            parts.append(
                jnp.concatenate([f3[2 * ai + p] for ai in range(first, first + count)], axis=0)
            )
        cpre = mm(jnp.concatenate(parts, axis=1), w_down[...], NN)
        sig = sigmoid(cpre)
        coarse = cpre * sig
        slope_c = sig * (1.0 + cpre * (1.0 - sig))
        grad_coarse = mm(c4[first : first + count].reshape(count * 32, 512), w_up[...], NT)
        grad = grad_coarse * slope_c
        ahead = pltpu.roll(grad, count * 32 - 1, 0)
        gs[first : first + count, :, 0:256] = grad.astype(BF).reshape(count, 32, 256)
        gs[first : first + count, :, 256:512] = ahead.astype(BF).reshape(count, 32, 256)
        low, high = max(first, 1), min(first + count, 17)
        inner = slice((low - first) * 32, (high - first) * 32)
        coarse_own[low - 1 : high - 1] = (
            (coarse[inner].reshape(high - low, 32, 256) * own[None]).astype(BF)
        )
        g_own[low - 1 : high - 1] = (
            (grad[inner].reshape(high - low, 32, 256) * own[None]).astype(BF)
        )

    for first in (0, 8):
        up = mm(coarse_own[first : first + 8].reshape(256, 256), w_up[...], NN)
        for a in range(first, first + 8):
            for p in range(2):
                for q in range(2):
                    k = 2 * p + q
                    value = up[(a - first) * 32 : (a - first + 1) * 32, k * 128 : (k + 1) * 128]
                    value = value + f3[2 * a + p + 3, :, 128 + q * 128 : 256 + q * 128].astype(F32)
                    mix[2 * a + p, pl.ds(4 + q, 32, stride=2), :] = value
    out[...] = mix[:, 8:64, :].astype(BF)
    coarse_flat = coarse_own[...].reshape(512, 256)
    res = mm(coarse_flat, c4[1:17].reshape(512, 512), TN)
    for k in range(4):
        up_acc[k * 256 : (k + 1) * 256, :] = res[:, k * 128 : (k + 1) * 128]
    g_flat = g_own[...].reshape(512, 256)
    for p in range(3):
        window = jnp.concatenate([f3[2 * a + p + 2] for a in range(16)], axis=0)
        res = mm(window, g_flat, TN)
        for side in range(2):
            down_acc[side, p * 384 : (p + 1) * 384, :] = res[:, side * 128 : (side + 1) * 128]

    for first, count in ((0, 9), (9, 8)):
        for odd in (True, False):
            here = gs[first : first + count].reshape(count * 32, 512)
            below = gs[first + 1 : first + 1 + count].reshape(count * 32, 512)
            if odd:
                spread = mm(jnp.concatenate([here, below], axis=1), w_odd[...], NT)
                cot = c4[first : first + count, :, 256:512].reshape(count * 32, 256)
                at = 2
            else:
                spread = mm(below, w_even[...], NT)
                cot = c4[first + 1 : first + 1 + count, :, 0:256].reshape(count * 32, 256)
                at = 3
            slopes = jnp.concatenate([slope[2 * ai + at] for ai in range(first, first + count)], 0)
            grad = (cot.astype(F32) + spread) * slopes
            grad = (grad.reshape(count, 32, 256) * in_grid[None]).reshape(count * 32, 256)
            if first == 0 and odd:
                row = lax.broadcasted_iota(jnp.int32, (count * 32, 256), 0)
                grad = jnp.where(row < 32, grad * keep_top, grad)
            if first != 0 and not odd:
                row = lax.broadcasted_iota(jnp.int32, (count * 32, 256), 0)
                grad = jnp.where(row >= (count - 1) * 32, grad * keep_bot, grad)
            behind = pltpu.roll(grad[:, 128:256], 1, 0).astype(BF)
            ahead = pltpu.roll(grad[:, 0:128], count * 32 - 1, 0).astype(BF)
            rounded = grad.astype(BF)
            kept = (grad.reshape(count, 32, 256) * own[None]).astype(BF)
            for ai in range(first, first + count):
                g_row = 2 * ai + (0 if odd else 1)
                rows = slice((ai - first) * 32, (ai - first + 1) * 32)
                g4[g_row, :, 0:128] = behind[rows]
                g4[g_row, :, 128:384] = rounded[rows]
                g4[g_row, :, 384:512] = ahead[rows]
                if 1 <= g_row <= 32:
                    pre_own[g_row - 1] = kept[ai - first]

    for first in (0, 8, 16, 24):
        total = None
        for p in range(3):
            window = g4[first + 2 - p : first + 10 - p].reshape(256, 512)
            term = mm(window, w_bwd[p], NT)
            total = term if total is None else total + term
        for i in range(first, first + 8):
            for q in range(2):
                mix[i, pl.ds(4 + q, 32, stride=2), :] = total[
                    (i - first) * 32 : (i - first + 1) * 32, q * 128 : (q + 1) * 128
                ]
    gx[...] = mix[:, 8:64, :].astype(BF)
    flat = pre_own[...].reshape(1024, 256)
    for p in range(3):
        res = mm(flat, x4[p + 3 : p + 35].reshape(1024, 512), TN)
        for q in range(3):
            tap = res[0:128, q * 128 : (q + 1) * 128] + res[128:256, (q + 1) * 128 : (q + 2) * 128]
            conv_acc[(3 * p + q) * 128 : (3 * p + q + 1) * 128, :] = tap.T

    @pl.when(edge[4] == 0)
    def _():
        pack(0, keep, conv_acc, down_acc, up_acc)
        pack(1, send, conv_acc, down_acc, up_acc)

    @pl.when(edge[4] != 0)
    def _():
        pack(1, keep, conv_acc, down_acc, up_acc)
        pack(0, send, conv_acc, down_acc, up_acc)


def level(edge, x, c, top, bot, left, right, weights, w_down):
    w_fwd, w_bwd, w_up, w_even, w_odd = weights
    vmem = pl.BlockSpec(memory_space=pltpu.VMEM)
    return pl.pallas_call(
        level_kernel,
        out_shape=(
            jax.ShapeDtypeStruct((32, 56, 128), BF),
            jax.ShapeDtypeStruct((32, 56, 128), BF),
            held((4, 640, 128)),
            held((4, 640, 128)),
        ),
        in_specs=[pl.BlockSpec(memory_space=pltpu.SMEM)] + [vmem] * 12,
        out_specs=(vmem,) * 4,
        scratch_shapes=[
            pltpu.VMEM((1160, 128), F32),
            pltpu.VMEM((2, 1160, 128), F32),
            pltpu.VMEM((1032, 128), F32),
            pltpu.VMEM((39, 72, 128), F32),
            pltpu.VMEM((36, 72, 128), F32),
            pltpu.VMEM((40, 32, 512), BF),
            pltpu.VMEM((18, 32, 512), BF),
            pltpu.VMEM((38, 32, 384), BF),
            pltpu.VMEM((38, 32, 256), F32),
            pltpu.VMEM((18, 32, 512), BF),
            pltpu.VMEM((16, 32, 256), BF),
            pltpu.VMEM((16, 32, 256), BF),
            pltpu.VMEM((34, 32, 512), BF),
            pltpu.VMEM((32, 32, 256), BF),
            pltpu.VMEM((32, 72, 128), F32),
        ],
        compiler_params=pltpu.CompilerParams(vmem_limit_bytes=18 * 1024 * 1024),
        name="level",
    )(
        edge, x, c, top, bot, *pin(left, right), w_fwd, w_bwd, w_down, w_up, w_even, w_odd
    )


def chain(axis, step):
    count = lax.axis_size(axis)
    return [(i, i + step) for i in range(count) if 0 <= i + step < count]


def rows_kernel(x_last, x_first, c_last, c_first, down, up):
    down[0:4] = x_last[...]
    down[4:6] = c_last[...]
    up[0:3] = x_first[0:3]
    up[3:5] = c_first[...]


def cols_kernel(
    x_last, x_first, c_last, c_first, top, bot, w_odd, right, left
):
    for out, cols, near, x, c in (
        (right, slice(52, 56), slice(4, 8), x_last, c_last),
        (left, slice(0, 4), slice(0, 4), x_first, c_first),
    ):
        out[0:4] = top[0:4, cols, :]
        out[4:36] = x[:, near, :]
        out[36:39] = bot[0:3, cols, :]
        out[39:41] = top[4:6, cols, :]
        out[41:73] = c[:, near, :]
        out[73:75] = bot[3:5, cols, :]


def row_block(count, at):
    return pl.BlockSpec((count, 56, 128), lambda i: (at, 0, 0))


def col_block(count, at):
    return pl.BlockSpec((count, 8, 128), lambda i: (0, at, 0))


def exchange(x, c, w_odd):
    down, up = pl.pallas_call(
        rows_kernel,
        grid=(1,),
        out_shape=(
            jax.ShapeDtypeStruct((6, 56, 128), BF),
            jax.ShapeDtypeStruct((5, 56, 128), BF),
        ),
        in_specs=[row_block(4, 7), row_block(4, 0), row_block(2, 15), row_block(2, 0)],
        out_specs=(row_block(6, 0), row_block(5, 0)),
        name="rows",
    )(*far(x, x, c, c))
    top = lax.ppermute(down, "row", chain("row", 1))
    bot = lax.ppermute(up, "row", chain("row", -1))
    whole = pl.BlockSpec((75, 4, 128), lambda i: (0, 0, 0))
    going_right, going_left = pl.pallas_call(
        cols_kernel,
        grid=(1,),
        out_shape=(jax.ShapeDtypeStruct((75, 4, 128), BF),) * 2,
        in_specs=[col_block(32, at) for at in (6, 0, 6, 0)]
        + [row_block(6, 0), row_block(5, 0), pl.BlockSpec(memory_space=pl.ANY)],
        out_specs=(whole, whole),
        name="cols",
    )(*far(x, x, c, c), *pin(top, bot), *far(w_odd))
    left = lax.ppermute(going_right, "col", chain("col", 1))
    right = lax.ppermute(going_left, "col", chain("col", -1))
    return top, bot, left, right


def local_terms(inputs, cotangent, w_conv, w_down, w_up):
    n_row, n_col = lax.axis_size("row"), lax.axis_size("col")
    at_row, at_col = lax.axis_index("row"), lax.axis_index("col")
    edge = jnp.array(
        [at_row == 0, at_row == n_row - 1, at_col == 0, at_col == n_col - 1, at_col & 1, at_col & 3]
    ).astype(jnp.int32)
    weights = prepare_weights(w_conv, w_down, w_up)
    halo = exchange(inputs, cotangent, weights[4])
    return edge, level(edge, inputs, cotangent, *halo, weights, w_down.reshape(1152, 256))


def spread_kernel(received, out, spare, total):
    total[0:640, :] = jnp.sum(received[...].astype(F32), axis=0)
    spare[...] = jnp.zeros((8, 128), F32)
    for z in range(8):
        for y in range(8):
            first = (y % 2) * 320 + z * 4 + y // 2
            out[8 * z + y] = total[pl.ds(first, 10, stride=32), :].astype(BF)


def finish_kernel(scale, edge, received, conv, down, up):
    rows = jnp.sum(received[...].astype(F32), axis=0) * scale
    for which in range(4):

        @pl.when(edge[5] == which)
        def _():
            for ref, base, names, size in (
                (conv, 0, CONV_ROWS, 288), (down, 3, DOWN_ROWS, 576), (up, 8, UP_ROWS, 256)
            ):
                start = (base - names[which][0]) * 128 + which * size
                done = 0
                while done < size:
                    row, lane = divmod(start + done, 128)
                    count = min(128 - lane, size - done)
                    ref[pl.ds(done, count)] = rows[row, lane : lane + count]
                    done += count


def coordinates():
    def device(x, y, z, core):
        return (x * 4 + z // 2) * 32 + (z % 2) * 16 + y * 2 + core

    across = [
        [device(x, y, z, k) for x in range(4)]
        for z in range(8) for y in range(8) for k in range(2)
    ]
    plane = [
        [device(x, y, z, k) for z in range(8) for y in range(8)]
        for x in range(4) for k in range(2)
    ]
    return across, plane


def reduce_owners(edge, keep, send, scale):
    mesh = ("row", "col")
    across, plane = coordinates()
    other = lax.ppermute(send, "col", [(i, i ^ 1) for i in range(32)])
    pair = (keep.astype(F32) + other.astype(F32)).astype(BF)
    got = lax.all_to_all(pair, mesh, 0, 0, axis_index_groups=across, tiled=True)
    spread, _ = pl.pallas_call(
        spread_kernel,
        out_shape=(held((64, 10, 128)), held((8, 128), F32)),
        scratch_shapes=[pltpu.VMEM((672, 128), F32)],
        name="spread",
    )(*pin(got))
    got = lax.all_to_all(spread, mesh, 0, 0, axis_index_groups=plane, tiled=True)
    sums = pl.pallas_call(
        functools.partial(finish_kernel, scale),
        out_shape=tuple(jax.ShapeDtypeStruct((n,), F32) for n in (288, 576, 256)),
        in_specs=[
            pl.BlockSpec(memory_space=pltpu.SMEM),
            pl.BlockSpec(memory_space=pltpu.VMEM),
        ],
        name="finish",
    )(edge, *pin(got))
    return sums


def body(inputs, cotangent, w_conv, w_down, w_up):
    edge, parts = local_terms(inputs, cotangent, w_conv, w_down, w_up)
    output, grad_inputs, keep, send = parts
    rows, cols, _ = inputs.shape
    scale = 1.0 / math.sqrt(rows * lax.axis_size("row") * cols * lax.axis_size("col"))
    return (output, grad_inputs, *reduce_owners(edge, keep, send, scale))


def solution(mesh):
    grid = P("row", "col", None)
    flat = P(("row", "col"))
    return jax.shard_map(
        body,
        mesh=mesh,
        in_specs=(grid, grid, P(), P(), P()),
        out_specs=(grid, grid, flat, flat, flat),
        check_vma=False,
    )
```

```python
import functools
import math

import jax
import jax.numpy as jnp
from jax import lax
from jax.experimental import pallas as pl
from jax.experimental.pallas import tpu as pltpu
from jax.sharding import PartitionSpec as P

BF = jnp.bfloat16
F32 = jnp.float32
NN = (((1,), (0,)), ((), ()))
NT = (((1,), (1,)), ((), ()))
TN = (((0,), (0,)), ((), ()))
SMALL = pltpu.CompilerParams(vmem_limit_bytes=8 * 1024 * 1024)


def held(shape, dtype=BF):
    return pltpu.VMEM(shape, dtype)


def far(*arrays):
    return tuple(pltpu.with_memory_space_constraint(a, pltpu.HBM) for a in arrays)


def pin(*arrays):
    return tuple(pltpu.with_memory_space_constraint(a, pltpu.VMEM) for a in arrays)


def swapped(odd, one, two):
    one, two = one[...].astype(F32), two[...].astype(F32)
    return jnp.where(odd, two, one), jnp.where(odd, one, two)


def mm(left, right, dims):
    return lax.dot_general(left, right, dims, preferred_element_type=F32)


def sigmoid(value):
    return 1.0 / (1.0 + jnp.exp(-value))


def weights_kernel(wc, wd, wu, conv_fwd, conv_bwd, up, down_even, down_odd):
    zero = jnp.zeros((128, 128), BF)
    for p in range(3):
        for blk in range(4):
            rows = slice(blk * 128, (blk + 1) * 128)
            conv_fwd[p, rows, 0:128] = wc[p, blk] if blk < 3 else zero
            conv_fwd[p, rows, 128:256] = wc[p, blk - 1] if blk > 0 else zero
            conv_bwd[p, 0:128, rows] = wc[p, 2 - blk] if blk < 3 else zero
            conv_bwd[p, 128:256, rows] = wc[p, 3 - blk] if blk > 0 else zero
    for p in range(2):
        for q in range(2):
            up[:, (2 * p + q) * 128 : (2 * p + q + 1) * 128] = wu[p, q]
    wide = jnp.zeros((128, 256), BF)
    down_even[0:128, 0:256] = wd[1, 1]
    down_even[0:128, 256:512] = wide
    down_even[128:256, 0:256] = wd[1, 2]
    down_even[128:256, 256:512] = wd[1, 0]
    down_odd[0:128, 0:256] = wd[2, 1]
    down_odd[0:128, 256:512] = wide
    down_odd[0:128, 512:768] = wd[0, 1]
    down_odd[0:128, 768:1024] = wide
    down_odd[128:256, 0:256] = wd[2, 2]
    down_odd[128:256, 256:512] = wd[2, 0]
    down_odd[128:256, 512:768] = wd[0, 2]
    down_odd[128:256, 768:1024] = wd[0, 0]


def prepare_weights(w_conv, w_down, w_up):
    shapes = ((3, 512, 256), (3, 256, 512), (256, 512), (256, 512), (256, 1024))
    return pl.pallas_call(
        weights_kernel,
        out_shape=tuple(held(s) for s in shapes),
        compiler_params=SMALL,
        name="weights",
    )(w_conv, w_down, w_up)


CONV_ROWS = ((0, 1, 2), (2, 3, 4), (4, 5, 6), (6, 7, 8))
DOWN_ROWS = ((0, 1, 2, 3, 4), (4, 5, 6, 7, 8), (9, 10, 11, 12, 13), (13, 14, 15, 16, 17))
UP_ROWS = ((0, 1), (2, 3), (4, 5), (6, 7))


def pack(core, ref, conv_acc, down_acc, up_acc):
    k = 0
    for owner in (core, core + 2):
        for row in CONV_ROWS[owner]:
            value = conv_acc[pl.ds(row, 128, stride=9), :]
            ref[:, 32 * k : 32 * k + 32, :] = value.reshape(4, 32, 128).astype(BF)
            k += 1
        for row in DOWN_ROWS[owner]:
            value = down_acc[row % 2, pl.ds(row // 2, 128, stride=9), :]
            ref[:, 32 * k : 32 * k + 32, :] = value.reshape(4, 32, 128).astype(BF)
            k += 1
        for row in UP_ROWS[owner]:
            value = up_acc[pl.ds(row, 128, stride=8), :]
            ref[:, 32 * k : 32 * k + 32, :] = value.reshape(4, 32, 128).astype(BF)
            k += 1


def level_kernel(
    x, c, row_a, row_b, col_a, col_b, w_fwd, w_bwd, w_down, w_up, w_even, w_odd,
    out, gx, keep, send,
    conv_acc, down_acc, up_acc, xs, cs, x4, c4, f3, slope, gs, coarse_own, g_own, g4, pre_own, mix,
):
    for ref in (xs, cs):
        ref[:, 0:8, :] = jnp.zeros((ref.shape[0], 8, 128), F32)
        ref[:, 64:72, :] = jnp.zeros((ref.shape[0], 8, 128), F32)
    at_row, at_col = lax.axis_index("row"), lax.axis_index("col")
    odd_row, odd_col = at_row % 2 == 1, at_col % 2 == 1
    top, bot = swapped(odd_row, row_b, row_a)
    left, right = swapped(odd_col, col_b, col_a)
    xs[4:36, 8:64, :] = x[...].astype(F32)
    xs[0:4, 8:64, :] = top[0:4]
    xs[36:39, 8:64, :] = bot[0:3]
    xs[0:39, 4:8, :] = left[0:39]
    xs[0:39, 64:68, :] = right[0:39]
    cs[2:34, 8:64, :] = c[...].astype(F32)
    cs[0:2, 8:64, :] = top[4:6]
    cs[34:36, 8:64, :] = bot[4:6]
    cs[0:36, 4:8, :] = left[39:75]
    cs[0:36, 64:68, :] = right[39:75]
    for r in range(39):
        for k in range(4):
            x4[r, :, k * 128 : (k + 1) * 128] = xs[r, pl.ds(3 + k, 32, stride=2), :].astype(BF)
    x4[39] = jnp.zeros((32, 512), BF)
    for ai in range(18):
        for p in range(2):
            for q in range(2):
                k = 2 * p + q
                c4[ai, :, k * 128 : (k + 1) * 128] = cs[
                    2 * ai + p, pl.ds(4 + q, 32, stride=2), :
                ].astype(BF)

    is_top, is_bot = at_row == 0, at_row == lax.axis_size("row") - 1
    is_left, is_right = at_col == 0, at_col == lax.axis_size("col") - 1
    half = lax.broadcasted_iota(jnp.int32, (32, 256), 0) - 2
    in_grid = ((half >= 0) | jnp.logical_not(is_left)) & ((half < 28) | jnp.logical_not(is_right))
    in_grid = jnp.where(in_grid, 1.0, 0.0)
    own = jnp.where((half >= 0) & (half < 28), 1.0, 0.0)
    keep_top = jnp.where(is_top, 0.0, 1.0)
    keep_bot = jnp.where(is_bot, 0.0, 1.0)

    for first, count in ((0, 8), (8, 8), (16, 8), (24, 8), (32, 6)):
        pre = None
        for p in range(3):
            window = x4[first + p : first + p + count].reshape(count * 32, 512)
            term = mm(window, w_fwd[p], NN)
            pre = term if pre is None else pre + term
        sig = sigmoid(pre)
        slope[first : first + count] = (sig * (1.0 + pre * (1.0 - sig))).reshape(count, 32, 256)
        fine = ((pre * sig).reshape(count, 32, 256) * in_grid[None]).reshape(count * 32, 256)
        if first == 0 or first == 32:
            row = lax.broadcasted_iota(jnp.int32, (count * 32, 256), 0) // 32
            if first == 0:
                fine = jnp.where(row < 3, fine * keep_top, fine)
            else:
                fine = jnp.where(row >= 3, fine * keep_bot, fine)
        rounded = fine.astype(BF).reshape(count, 32, 256)
        behind = pltpu.roll(fine[:, 128:256], 1, 0).astype(BF).reshape(count, 32, 128)
        f3[first : first + count, :, 0:128] = behind
        f3[first : first + count, :, 128:384] = rounded

    for first, count in ((0, 9), (9, 9)):
        parts = []
        for p in range(3):
            parts.append(
                jnp.concatenate([f3[2 * ai + p] for ai in range(first, first + count)], axis=0)
            )
        cpre = mm(jnp.concatenate(parts, axis=1), w_down[...], NN)
        sig = sigmoid(cpre)
        coarse = cpre * sig
        slope_c = sig * (1.0 + cpre * (1.0 - sig))
        grad_coarse = mm(c4[first : first + count].reshape(count * 32, 512), w_up[...], NT)
        grad = grad_coarse * slope_c
        ahead = pltpu.roll(grad, count * 32 - 1, 0)
        gs[first : first + count, :, 0:256] = grad.astype(BF).reshape(count, 32, 256)
        gs[first : first + count, :, 256:512] = ahead.astype(BF).reshape(count, 32, 256)
        low, high = max(first, 1), min(first + count, 17)
        inner = slice((low - first) * 32, (high - first) * 32)
        coarse_own[low - 1 : high - 1] = (
            (coarse[inner].reshape(high - low, 32, 256) * own[None]).astype(BF)
        )
        g_own[low - 1 : high - 1] = (
            (grad[inner].reshape(high - low, 32, 256) * own[None]).astype(BF)
        )

    for first in (0, 8):
        up = mm(coarse_own[first : first + 8].reshape(256, 256), w_up[...], NN)
        for a in range(first, first + 8):
            for p in range(2):
                for q in range(2):
                    k = 2 * p + q
                    value = up[(a - first) * 32 : (a - first + 1) * 32, k * 128 : (k + 1) * 128]
                    value = value + f3[2 * a + p + 3, :, 128 + q * 128 : 256 + q * 128].astype(F32)
                    mix[2 * a + p, pl.ds(4 + q, 32, stride=2), :] = value
    out[...] = mix[:, 8:64, :].astype(BF)
    coarse_flat = coarse_own[...].reshape(512, 256)
    res = mm(coarse_flat, c4[1:17].reshape(512, 512), TN)
    for k in range(4):
        up_acc[k * 256 : (k + 1) * 256, :] = res[:, k * 128 : (k + 1) * 128]
    g_flat = g_own[...].reshape(512, 256)
    for p in range(3):
        window = jnp.concatenate([f3[2 * a + p + 2] for a in range(16)], axis=0)
        res = mm(window, g_flat, TN)
        for side in range(2):
            down_acc[side, p * 384 : (p + 1) * 384, :] = res[:, side * 128 : (side + 1) * 128]

    for first, count in ((0, 9), (9, 8)):
        for odd in (True, False):
            here = gs[first : first + count].reshape(count * 32, 512)
            below = gs[first + 1 : first + 1 + count].reshape(count * 32, 512)
            if odd:
                spread = mm(jnp.concatenate([here, below], axis=1), w_odd[...], NT)
                cot = c4[first : first + count, :, 256:512].reshape(count * 32, 256)
                at = 2
            else:
                spread = mm(below, w_even[...], NT)
                cot = c4[first + 1 : first + 1 + count, :, 0:256].reshape(count * 32, 256)
                at = 3
            slopes = jnp.concatenate([slope[2 * ai + at] for ai in range(first, first + count)], 0)
            grad = (cot.astype(F32) + spread) * slopes
            grad = (grad.reshape(count, 32, 256) * in_grid[None]).reshape(count * 32, 256)
            if first == 0 and odd:
                row = lax.broadcasted_iota(jnp.int32, (count * 32, 256), 0)
                grad = jnp.where(row < 32, grad * keep_top, grad)
            if first != 0 and not odd:
                row = lax.broadcasted_iota(jnp.int32, (count * 32, 256), 0)
                grad = jnp.where(row >= (count - 1) * 32, grad * keep_bot, grad)
            behind = pltpu.roll(grad[:, 128:256], 1, 0).astype(BF)
            ahead = pltpu.roll(grad[:, 0:128], count * 32 - 1, 0).astype(BF)
            rounded = grad.astype(BF)
            kept = (grad.reshape(count, 32, 256) * own[None]).astype(BF)
            for ai in range(first, first + count):
                g_row = 2 * ai + (0 if odd else 1)
                rows = slice((ai - first) * 32, (ai - first + 1) * 32)
                g4[g_row, :, 0:128] = behind[rows]
                g4[g_row, :, 128:384] = rounded[rows]
                g4[g_row, :, 384:512] = ahead[rows]
                if 1 <= g_row <= 32:
                    pre_own[g_row - 1] = kept[ai - first]

    for first in (0, 8, 16, 24):
        total = None
        for p in range(3):
            window = g4[first + 2 - p : first + 10 - p].reshape(256, 512)
            term = mm(window, w_bwd[p], NT)
            total = term if total is None else total + term
        for i in range(first, first + 8):
            for q in range(2):
                mix[i, pl.ds(4 + q, 32, stride=2), :] = total[
                    (i - first) * 32 : (i - first + 1) * 32, q * 128 : (q + 1) * 128
                ]
    gx[...] = mix[:, 8:64, :].astype(BF)
    flat = pre_own[...].reshape(1024, 256)
    for p in range(3):
        res = mm(flat, x4[p + 3 : p + 35].reshape(1024, 512), TN)
        for q in range(3):
            tap = res[0:128, q * 128 : (q + 1) * 128] + res[128:256, (q + 1) * 128 : (q + 2) * 128]
            conv_acc[(3 * p + q) * 128 : (3 * p + q + 1) * 128, :] = tap.T

    @pl.when(jnp.logical_not(odd_col))
    def _():
        pack(0, keep, conv_acc, down_acc, up_acc)
        pack(1, send, conv_acc, down_acc, up_acc)

    @pl.when(odd_col)
    def _():
        pack(1, keep, conv_acc, down_acc, up_acc)
        pack(0, send, conv_acc, down_acc, up_acc)


def level(x, c, halo, weights, w_down):
    w_fwd, w_bwd, w_up, w_even, w_odd = weights
    vmem = pl.BlockSpec(memory_space=pltpu.VMEM)
    return pl.pallas_call(
        level_kernel,
        out_shape=(
            jax.ShapeDtypeStruct((32, 56, 128), BF),
            jax.ShapeDtypeStruct((32, 56, 128), BF),
            held((4, 640, 128)),
            held((4, 640, 128)),
        ),
        in_specs=[vmem] * 12,
        out_specs=(vmem,) * 4,
        scratch_shapes=[
            pltpu.VMEM((1160, 128), F32),
            pltpu.VMEM((2, 1160, 128), F32),
            pltpu.VMEM((1032, 128), F32),
            pltpu.VMEM((39, 72, 128), F32),
            pltpu.VMEM((36, 72, 128), F32),
            pltpu.VMEM((40, 32, 512), BF),
            pltpu.VMEM((18, 32, 512), BF),
            pltpu.VMEM((38, 32, 384), BF),
            pltpu.VMEM((38, 32, 256), F32),
            pltpu.VMEM((18, 32, 512), BF),
            pltpu.VMEM((16, 32, 256), BF),
            pltpu.VMEM((16, 32, 256), BF),
            pltpu.VMEM((34, 32, 512), BF),
            pltpu.VMEM((32, 32, 256), BF),
            pltpu.VMEM((32, 72, 128), F32),
        ],
        compiler_params=pltpu.CompilerParams(vmem_limit_bytes=18 * 1024 * 1024),
        name="level",
    )(
        x, c, *halo[:2], *pin(*halo[2:]), *pin(w_fwd, w_bwd), w_down, *pin(w_up, w_even, w_odd)
    )


def pairs(axis):
    count = lax.axis_size(axis)
    both = []
    for first in (0, 1):
        swaps = [(i, i + 1) for i in range(first, count - 1, 2)]
        both.append(swaps + [(b, a) for a, b in swaps])
    return both


def store_pair(odd, forward, backward, even_first, odd_first):
    even_first[...] = jnp.where(odd, backward, forward).astype(BF)
    odd_first[...] = jnp.where(odd, forward, backward).astype(BF)


def rows_kernel(x_last, x_first, c_last, c_first, row_a, row_b):
    odd = lax.axis_index("row") % 2 == 1
    down = jnp.concatenate([x_last[...], c_last[...]], axis=0).astype(F32)
    up = jnp.concatenate([x_first[...], c_first[...]], axis=0).astype(F32)
    store_pair(odd, down, up, row_a, row_b)


def cols_kernel(x_last, x_first, c_last, c_first, row_a, row_b, col_a, col_b):
    top, bot = swapped(lax.axis_index("row") % 2 == 1, row_b, row_a)

    def side(cols, near, x, c):
        x, c = x[...].astype(F32), c[...].astype(F32)
        return jnp.concatenate(
            [
                top[0:4, cols], x[:, near], bot[0:3, cols],
                top[4:6, cols], c[:, near], bot[4:6, cols],
            ],
            axis=0,
        )

    rightward = side(slice(52, 56), slice(4, 8), x_last, c_last)
    leftward = side(slice(0, 4), slice(0, 4), x_first, c_first)
    store_pair(lax.axis_index("col") % 2 == 1, rightward, leftward, col_a, col_b)


def row_block(count, at):
    return pl.BlockSpec((count, 56, 128), lambda i: (at, 0, 0))


def col_block(count, at):
    return pl.BlockSpec((count, 8, 128), lambda i: (0, at, 0))


def exchange(x, c):
    first, second = pl.pallas_call(
        rows_kernel,
        grid=(1,),
        out_shape=(jax.ShapeDtypeStruct((6, 56, 128), BF),) * 2,
        in_specs=[row_block(4, 7), row_block(4, 0), row_block(2, 15), row_block(2, 0)],
        out_specs=(row_block(6, 0),) * 2,
        compiler_params=SMALL,
        name="rows",
    )(*far(x, x, c, c))
    even, odd = pairs("row")
    row_a = lax.ppermute(first, "row", even)
    row_b = lax.ppermute(second, "row", odd)
    whole = pl.BlockSpec((75, 4, 128), lambda i: (0, 0, 0))
    first, second = pl.pallas_call(
        cols_kernel,
        grid=(1,),
        out_shape=(jax.ShapeDtypeStruct((75, 4, 128), BF),) * 2,
        in_specs=[col_block(32, at) for at in (6, 0, 6, 0)] + [row_block(6, 0)] * 2,
        out_specs=(whole, whole),
        compiler_params=SMALL,
        name="cols",
    )(*far(x, x, c, c), *pin(row_a, row_b))
    even, odd = pairs("col")
    col_a = lax.ppermute(first, "col", even)
    col_b = lax.ppermute(second, "col", odd)
    return row_a, row_b, col_a, col_b


def local_terms(inputs, cotangent, w_conv, w_down, w_up):
    halo = exchange(inputs, cotangent)
    late_conv, _ = lax.optimization_barrier((w_conv, halo[0]))
    weights = prepare_weights(late_conv, w_down, w_up)
    return level(inputs, cotangent, halo, weights, w_down.reshape(1152, 256))


def spread_kernel(received, out, spare, total):
    total[0:640, :] = jnp.sum(received[...].astype(F32), axis=0)
    spare[...] = jnp.zeros((8, 128), F32)
    for z in range(8):
        for y in range(8):
            first = (y % 2) * 320 + z * 4 + y // 2
            out[8 * z + y] = total[pl.ds(first, 10, stride=32), :].astype(BF)


def finish_kernel(scale, received, conv, down, up):
    rows = jnp.sum(received[...].astype(F32), axis=0) * scale
    for which in range(4):

        @pl.when(lax.axis_index("col") % 4 == which)
        def _():
            for ref, base, names, size in (
                (conv, 0, CONV_ROWS, 288), (down, 3, DOWN_ROWS, 576), (up, 8, UP_ROWS, 256)
            ):
                start = (base - names[which][0]) * 128 + which * size
                done = 0
                while done < size:
                    row, lane = divmod(start + done, 128)
                    count = min(128 - lane, size - done)
                    ref[pl.ds(done, count)] = rows[row, lane : lane + count]
                    done += count


def coordinates():
    def device(x, y, z, core):
        return (x * 4 + z // 2) * 32 + (z % 2) * 16 + y * 2 + core

    across = [
        [device(x, y, z, k) for x in range(4)]
        for z in range(8) for y in range(8) for k in range(2)
    ]
    plane = [
        [device(x, y, z, k) for z in range(8) for y in range(8)]
        for x in range(4) for k in range(2)
    ]
    return across, plane


def reduce_owners(keep, send, scale):
    mesh = ("row", "col")
    across, plane = coordinates()
    other = lax.ppermute(send, "col", [(i, i ^ 1) for i in range(32)])
    pair = (keep.astype(F32) + other.astype(F32)).astype(BF)
    got = lax.all_to_all(pair, mesh, 0, 0, axis_index_groups=across, tiled=True)
    spread, _ = pl.pallas_call(
        spread_kernel,
        out_shape=(held((64, 10, 128)), held((8, 128), F32)),
        scratch_shapes=[pltpu.VMEM((672, 128), F32)],
        compiler_params=SMALL,
        name="spread",
    )(*pin(got))
    got = lax.all_to_all(spread, mesh, 0, 0, axis_index_groups=plane, tiled=True)
    sums = pl.pallas_call(
        functools.partial(finish_kernel, scale),
        out_shape=tuple(jax.ShapeDtypeStruct((n,), F32) for n in (288, 576, 256)),
        compiler_params=SMALL,
        name="finish",
    )(*pin(got))
    return sums


def body(inputs, cotangent, w_conv, w_down, w_up):
    output, grad_inputs, keep, send = local_terms(inputs, cotangent, w_conv, w_down, w_up)
    rows, cols, _ = inputs.shape
    scale = 1.0 / math.sqrt(rows * lax.axis_size("row") * cols * lax.axis_size("col"))
    return (output, grad_inputs, *reduce_owners(keep, send, scale))


def solution(mesh):
    grid = P("row", "col", None)
    flat = P(("row", "col"))
    return jax.shard_map(
        body,
        mesh=mesh,
        in_specs=(grid, grid, P(), P(), P()),
        out_specs=(grid, grid, flat, flat, flat),
        check_vma=False,
    )
```

```python
import functools
import math

import jax
import jax.numpy as jnp
from jax import lax
from jax.experimental import pallas as pl
from jax.experimental.pallas import tpu as pltpu
from jax.sharding import PartitionSpec as P

BF = jnp.bfloat16
F32 = jnp.float32
NN = (((1,), (0,)), ((), ()))
NT = (((1,), (1,)), ((), ()))
TN = (((0,), (0,)), ((), ()))
SMALL = pltpu.CompilerParams(vmem_limit_bytes=8 * 1024 * 1024)


def held(shape, dtype=BF):
    return pltpu.VMEM(shape, dtype)


def far(*arrays):
    return tuple(pltpu.with_memory_space_constraint(a, pltpu.HBM) for a in arrays)


def pin(*arrays):
    return tuple(pltpu.with_memory_space_constraint(a, pltpu.VMEM) for a in arrays)


def swapped(odd, one, two):
    one, two = one[...].astype(F32), two[...].astype(F32)
    return jnp.where(odd, two, one), jnp.where(odd, one, two)


def mm(left, right, dims):
    return lax.dot_general(left, right, dims, preferred_element_type=F32)


def sigmoid(value):
    return 1.0 / (1.0 + jnp.exp(-value))


def weights_kernel(wc, wd, wu, conv_fwd, conv_bwd, up, down_even, down_odd):
    zero = jnp.zeros((128, 128), BF)
    for p in range(3):
        for blk in range(4):
            rows = slice(blk * 128, (blk + 1) * 128)
            conv_fwd[p, rows, 0:128] = wc[p, blk] if blk < 3 else zero
            conv_fwd[p, rows, 128:256] = wc[p, blk - 1] if blk > 0 else zero
            conv_bwd[p, 0:128, rows] = wc[p, 2 - blk] if blk < 3 else zero
            conv_bwd[p, 128:256, rows] = wc[p, 3 - blk] if blk > 0 else zero
    for p in range(2):
        for q in range(2):
            up[:, (2 * p + q) * 128 : (2 * p + q + 1) * 128] = wu[p, q]
    wide = jnp.zeros((128, 256), BF)
    down_even[0:128, 0:256] = wd[1, 1]
    down_even[0:128, 256:512] = wide
    down_even[128:256, 0:256] = wd[1, 2]
    down_even[128:256, 256:512] = wd[1, 0]
    down_odd[0:128, 0:256] = wd[2, 1]
    down_odd[0:128, 256:512] = wide
    down_odd[0:128, 512:768] = wd[0, 1]
    down_odd[0:128, 768:1024] = wide
    down_odd[128:256, 0:256] = wd[2, 2]
    down_odd[128:256, 256:512] = wd[2, 0]
    down_odd[128:256, 512:768] = wd[0, 2]
    down_odd[128:256, 768:1024] = wd[0, 0]


def prepare_weights(w_conv, w_down, w_up):
    shapes = ((3, 512, 256), (3, 256, 512), (256, 512), (256, 512), (256, 1024))
    return pl.pallas_call(
        weights_kernel,
        out_shape=tuple(held(s) for s in shapes),
        compiler_params=SMALL,
        name="weights",
    )(w_conv, w_down, w_up)


CONV_ROWS = ((0, 1, 2), (2, 3, 4), (4, 5, 6), (6, 7, 8))
DOWN_ROWS = ((0, 1, 2, 3, 4), (4, 5, 6, 7, 8), (9, 10, 11, 12, 13), (13, 14, 15, 16, 17))
UP_ROWS = ((0, 1), (2, 3), (4, 5), (6, 7))


def pack(core, ref, conv_acc, down_acc, up_acc):
    k = 0
    for owner in (core, core + 2):
        for row in CONV_ROWS[owner]:
            value = conv_acc[pl.ds(row, 128, stride=9), :]
            ref[:, 32 * k : 32 * k + 32, :] = value.reshape(4, 32, 128).astype(BF)
            k += 1
        for row in DOWN_ROWS[owner]:
            value = down_acc[row % 2, pl.ds(row // 2, 128, stride=9), :]
            ref[:, 32 * k : 32 * k + 32, :] = value.reshape(4, 32, 128).astype(BF)
            k += 1
        for row in UP_ROWS[owner]:
            value = up_acc[pl.ds(row, 128, stride=8), :]
            ref[:, 32 * k : 32 * k + 32, :] = value.reshape(4, 32, 128).astype(BF)
            k += 1


def level_kernel(
    x, c, row_a, row_b, col_a, col_b, w_fwd, w_down, w_up, w_even, w_odd,
    keep, send, f3, coarse_own, g4,
    conv_acc, down_acc, up_acc, xs, cs, x4, c4, slope, gs, g_own, pre_own,
):
    for ref in (xs, cs):
        ref[:, 0:8, :] = jnp.zeros((ref.shape[0], 8, 128), F32)
        ref[:, 64:72, :] = jnp.zeros((ref.shape[0], 8, 128), F32)
    at_row, at_col = lax.axis_index("row"), lax.axis_index("col")
    odd_row, odd_col = at_row % 2 == 1, at_col % 2 == 1
    top, bot = swapped(odd_row, row_b, row_a)
    left, right = swapped(odd_col, col_b, col_a)
    xs[4:36, 8:64, :] = x[...].astype(F32)
    xs[0:4, 8:64, :] = top[0:4]
    xs[36:39, 8:64, :] = bot[0:3]
    xs[0:39, 4:8, :] = left[0:39]
    xs[0:39, 64:68, :] = right[0:39]
    cs[2:34, 8:64, :] = c[...].astype(F32)
    cs[0:2, 8:64, :] = top[4:6]
    cs[34:36, 8:64, :] = bot[4:6]
    cs[0:36, 4:8, :] = left[39:75]
    cs[0:36, 64:68, :] = right[39:75]
    for r in range(39):
        for k in range(4):
            x4[r, :, k * 128 : (k + 1) * 128] = xs[r, pl.ds(3 + k, 32, stride=2), :].astype(BF)
    x4[39] = jnp.zeros((32, 512), BF)
    for ai in range(18):
        for p in range(2):
            for q in range(2):
                k = 2 * p + q
                c4[ai, :, k * 128 : (k + 1) * 128] = cs[
                    2 * ai + p, pl.ds(4 + q, 32, stride=2), :
                ].astype(BF)

    is_top, is_bot = at_row == 0, at_row == lax.axis_size("row") - 1
    is_left, is_right = at_col == 0, at_col == lax.axis_size("col") - 1
    half = lax.broadcasted_iota(jnp.int32, (32, 256), 0) - 2
    in_grid = ((half >= 0) | jnp.logical_not(is_left)) & ((half < 28) | jnp.logical_not(is_right))
    in_grid = jnp.where(in_grid, 1.0, 0.0)
    own = jnp.where((half >= 0) & (half < 28), 1.0, 0.0)
    keep_top = jnp.where(is_top, 0.0, 1.0)
    keep_bot = jnp.where(is_bot, 0.0, 1.0)

    for first, count in ((0, 8), (8, 8), (16, 8), (24, 8), (32, 6)):
        pre = None
        for p in range(3):
            window = x4[first + p : first + p + count].reshape(count * 32, 512)
            term = mm(window, w_fwd[p], NN)
            pre = term if pre is None else pre + term
        sig = sigmoid(pre)
        slope[first : first + count] = (sig * (1.0 + pre * (1.0 - sig))).reshape(count, 32, 256)
        fine = ((pre * sig).reshape(count, 32, 256) * in_grid[None]).reshape(count * 32, 256)
        if first == 0 or first == 32:
            row = lax.broadcasted_iota(jnp.int32, (count * 32, 256), 0) // 32
            if first == 0:
                fine = jnp.where(row < 3, fine * keep_top, fine)
            else:
                fine = jnp.where(row >= 3, fine * keep_bot, fine)
        rounded = fine.astype(BF).reshape(count, 32, 256)
        behind = pltpu.roll(fine[:, 128:256], 1, 0).astype(BF).reshape(count, 32, 128)
        f3[first : first + count, :, 0:128] = behind
        f3[first : first + count, :, 128:384] = rounded

    for first, count in ((0, 9), (9, 9)):
        parts = []
        for p in range(3):
            parts.append(
                jnp.concatenate([f3[2 * ai + p] for ai in range(first, first + count)], axis=0)
            )
        cpre = mm(jnp.concatenate(parts, axis=1), w_down[...], NN)
        sig = sigmoid(cpre)
        coarse = cpre * sig
        slope_c = sig * (1.0 + cpre * (1.0 - sig))
        grad_coarse = mm(c4[first : first + count].reshape(count * 32, 512), w_up[...], NT)
        grad = grad_coarse * slope_c
        ahead = pltpu.roll(grad, count * 32 - 1, 0)
        gs[first : first + count, :, 0:256] = grad.astype(BF).reshape(count, 32, 256)
        gs[first : first + count, :, 256:512] = ahead.astype(BF).reshape(count, 32, 256)
        low, high = max(first, 1), min(first + count, 17)
        inner = slice((low - first) * 32, (high - first) * 32)
        coarse_own[low - 1 : high - 1] = (
            (coarse[inner].reshape(high - low, 32, 256) * own[None]).astype(BF)
        )
        g_own[low - 1 : high - 1] = (
            (grad[inner].reshape(high - low, 32, 256) * own[None]).astype(BF)
        )

    coarse_flat = coarse_own[...].reshape(512, 256)
    res = mm(coarse_flat, c4[1:17].reshape(512, 512), TN)
    for k in range(4):
        up_acc[k * 256 : (k + 1) * 256, :] = res[:, k * 128 : (k + 1) * 128]
    g_flat = g_own[...].reshape(512, 256)
    for p in range(3):
        window = jnp.concatenate([f3[2 * a + p + 2] for a in range(16)], axis=0)
        res = mm(window, g_flat, TN)
        for side in range(2):
            down_acc[side, p * 384 : (p + 1) * 384, :] = res[:, side * 128 : (side + 1) * 128]

    for first, count in ((0, 9), (9, 8)):
        for odd in (True, False):
            here = gs[first : first + count].reshape(count * 32, 512)
            below = gs[first + 1 : first + 1 + count].reshape(count * 32, 512)
            if odd:
                spread = mm(jnp.concatenate([here, below], axis=1), w_odd[...], NT)
                cot = c4[first : first + count, :, 256:512].reshape(count * 32, 256)
                at = 2
            else:
                spread = mm(below, w_even[...], NT)
                cot = c4[first + 1 : first + 1 + count, :, 0:256].reshape(count * 32, 256)
                at = 3
            slopes = jnp.concatenate([slope[2 * ai + at] for ai in range(first, first + count)], 0)
            grad = (cot.astype(F32) + spread) * slopes
            grad = (grad.reshape(count, 32, 256) * in_grid[None]).reshape(count * 32, 256)
            if first == 0 and odd:
                row = lax.broadcasted_iota(jnp.int32, (count * 32, 256), 0)
                grad = jnp.where(row < 32, grad * keep_top, grad)
            if first != 0 and not odd:
                row = lax.broadcasted_iota(jnp.int32, (count * 32, 256), 0)
                grad = jnp.where(row >= (count - 1) * 32, grad * keep_bot, grad)
            behind = pltpu.roll(grad[:, 128:256], 1, 0).astype(BF)
            ahead = pltpu.roll(grad[:, 0:128], count * 32 - 1, 0).astype(BF)
            rounded = grad.astype(BF)
            kept = (grad.reshape(count, 32, 256) * own[None]).astype(BF)
            for ai in range(first, first + count):
                g_row = 2 * ai + (0 if odd else 1)
                rows = slice((ai - first) * 32, (ai - first + 1) * 32)
                g4[g_row, :, 0:128] = behind[rows]
                g4[g_row, :, 128:384] = rounded[rows]
                g4[g_row, :, 384:512] = ahead[rows]
                if 1 <= g_row <= 32:
                    pre_own[g_row - 1] = kept[ai - first]

    flat = pre_own[...].reshape(1024, 256)
    for p in range(3):
        res = mm(flat, x4[p + 3 : p + 35].reshape(1024, 512), TN)
        for q in range(3):
            tap = res[0:128, q * 128 : (q + 1) * 128] + res[128:256, (q + 1) * 128 : (q + 2) * 128]
            conv_acc[(3 * p + q) * 128 : (3 * p + q + 1) * 128, :] = tap.T

    @pl.when(jnp.logical_not(odd_col))
    def _():
        pack(0, keep, conv_acc, down_acc, up_acc)
        pack(1, send, conv_acc, down_acc, up_acc)

    @pl.when(odd_col)
    def _():
        pack(1, keep, conv_acc, down_acc, up_acc)
        pack(0, send, conv_acc, down_acc, up_acc)


def late_kernel(f3, coarse_own, g4, w_up, w_bwd, out, gx, mix):
    for first in (0, 8):
        up = mm(coarse_own[first : first + 8].reshape(256, 256), w_up[...], NN)
        for a in range(first, first + 8):
            for p in range(2):
                for q in range(2):
                    k = 2 * p + q
                    value = up[(a - first) * 32 : (a - first + 1) * 32, k * 128 : (k + 1) * 128]
                    value = value + f3[2 * a + p + 3, :, 128 + q * 128 : 256 + q * 128].astype(F32)
                    mix[2 * a + p, pl.ds(4 + q, 32, stride=2), :] = value
    out[...] = mix[:, 8:64, :].astype(BF)
    for first in (0, 8, 16, 24):
        total = None
        for p in range(3):
            window = g4[first + 2 - p : first + 10 - p].reshape(256, 512)
            term = mm(window, w_bwd[p], NT)
            total = term if total is None else total + term
        for i in range(first, first + 8):
            for q in range(2):
                mix[i, pl.ds(4 + q, 32, stride=2), :] = total[
                    (i - first) * 32 : (i - first + 1) * 32, q * 128 : (q + 1) * 128
                ]
    gx[...] = mix[:, 8:64, :].astype(BF)


def level(x, c, halo, weights, w_down):
    w_fwd, w_bwd, w_up, w_even, w_odd = weights
    vmem = pl.BlockSpec(memory_space=pltpu.VMEM)
    return pl.pallas_call(
        level_kernel,
        out_shape=(
            held((4, 640, 128)),
            held((4, 640, 128)),
            held((38, 32, 384)),
            held((16, 32, 256)),
            held((34, 32, 512)),
        ),
        in_specs=[vmem] * 11,
        out_specs=(vmem,) * 5,
        scratch_shapes=[
            pltpu.VMEM((1160, 128), F32),
            pltpu.VMEM((2, 1160, 128), F32),
            pltpu.VMEM((1032, 128), F32),
            pltpu.VMEM((39, 72, 128), F32),
            pltpu.VMEM((36, 72, 128), F32),
            pltpu.VMEM((40, 32, 512), BF),
            pltpu.VMEM((18, 32, 512), BF),
            pltpu.VMEM((38, 32, 256), F32),
            pltpu.VMEM((18, 32, 512), BF),
            pltpu.VMEM((16, 32, 256), BF),
            pltpu.VMEM((32, 32, 256), BF),
        ],
        compiler_params=pltpu.CompilerParams(vmem_limit_bytes=16 * 1024 * 1024),
        name="level",
    )(
        x, c, *halo[:2], *pin(*halo[2:]), *pin(w_fwd), w_down, *pin(w_up, w_even, w_odd)
    )


def late(f3, coarse_own, g4, w_up, w_bwd):
    return pl.pallas_call(
        late_kernel,
        out_shape=(jax.ShapeDtypeStruct((32, 56, 128), BF),) * 2,
        scratch_shapes=[pltpu.VMEM((32, 72, 128), F32)],
        compiler_params=SMALL,
        name="late",
    )(*pin(f3, coarse_own, g4, w_up, w_bwd))


def pairs(axis):
    count = lax.axis_size(axis)
    both = []
    for first in (0, 1):
        swaps = [(i, i + 1) for i in range(first, count - 1, 2)]
        both.append(swaps + [(b, a) for a, b in swaps])
    return both


def store_pair(odd, forward, backward, even_first, odd_first):
    even_first[...] = jnp.where(odd, backward, forward).astype(BF)
    odd_first[...] = jnp.where(odd, forward, backward).astype(BF)


def rows_kernel(x_last, x_first, c_last, c_first, row_a, row_b):
    odd = lax.axis_index("row") % 2 == 1
    down = jnp.concatenate([x_last[...], c_last[...]], axis=0).astype(F32)
    up = jnp.concatenate([x_first[...], c_first[...]], axis=0).astype(F32)
    store_pair(odd, down, up, row_a, row_b)


def cols_kernel(x_last, x_first, c_last, c_first, row_a, row_b, col_a, col_b):
    top, bot = swapped(lax.axis_index("row") % 2 == 1, row_b, row_a)

    def side(cols, near, x, c):
        x, c = x[...].astype(F32), c[...].astype(F32)
        return jnp.concatenate(
            [
                top[0:4, cols], x[:, near], bot[0:3, cols],
                top[4:6, cols], c[:, near], bot[4:6, cols],
            ],
            axis=0,
        )

    rightward = side(slice(52, 56), slice(4, 8), x_last, c_last)
    leftward = side(slice(0, 4), slice(0, 4), x_first, c_first)
    store_pair(lax.axis_index("col") % 2 == 1, rightward, leftward, col_a, col_b)


def row_block(count, at):
    return pl.BlockSpec((count, 56, 128), lambda i: (at, 0, 0))


def col_block(count, at):
    return pl.BlockSpec((count, 8, 128), lambda i: (0, at, 0))


def exchange(x, c):
    first, second = pl.pallas_call(
        rows_kernel,
        grid=(1,),
        out_shape=(jax.ShapeDtypeStruct((6, 56, 128), BF),) * 2,
        in_specs=[row_block(4, 7), row_block(4, 0), row_block(2, 15), row_block(2, 0)],
        out_specs=(row_block(6, 0),) * 2,
        compiler_params=SMALL,
        name="rows",
    )(*far(x, x, c, c))
    even, odd = pairs("row")
    row_a = lax.ppermute(first, "row", even)
    row_b = lax.ppermute(second, "row", odd)
    whole = pl.BlockSpec((75, 4, 128), lambda i: (0, 0, 0))
    first, second = pl.pallas_call(
        cols_kernel,
        grid=(1,),
        out_shape=(jax.ShapeDtypeStruct((75, 4, 128), BF),) * 2,
        in_specs=[col_block(32, at) for at in (6, 0, 6, 0)] + [row_block(6, 0)] * 2,
        out_specs=(whole, whole),
        compiler_params=SMALL,
        name="cols",
    )(*far(x, x, c, c), *pin(row_a, row_b))
    even, odd = pairs("col")
    col_a = lax.ppermute(first, "col", even)
    col_b = lax.ppermute(second, "col", odd)
    return row_a, row_b, col_a, col_b


def local_terms(inputs, cotangent, w_conv, w_down, w_up):
    halo = exchange(inputs, cotangent)
    late_conv, _ = lax.optimization_barrier((w_conv, halo[0]))
    weights = prepare_weights(late_conv, w_down, w_up)
    keep, send, *rest = level(inputs, cotangent, halo, weights, w_down.reshape(1152, 256))
    return keep, send, (*rest, weights[2], weights[1])


def spread_kernel(received, out, spare, total, stage):
    total[...] = jnp.sum(received[...].astype(F32), axis=0)
    spare[...] = jnp.zeros((8, 128), F32)
    for k in range(20):
        first = (k // 10) * 320 + k % 10
        stage[pl.ds(first, 32, stride=10), :] = total[32 * k : 32 * k + 32, :]
    out[...] = stage[0:640, :].astype(BF)


def finish_kernel(scale, received, conv, down, up, stage):
    total = received[0:80, :].astype(F32)
    for chunk in range(1, 8):
        total = total + received[80 * chunk : 80 * chunk + 80, :].astype(F32)
    stage[...] = total
    rows = stage[0:10, :]
    for holder in range(1, 8):
        rows = rows + stage[10 * holder : 10 * holder + 10, :]
    rows = rows * scale
    for which in range(4):

        @pl.when(lax.axis_index("col") % 4 == which)
        def _():
            for ref, base, names, size in (
                (conv, 0, CONV_ROWS, 288), (down, 3, DOWN_ROWS, 576), (up, 8, UP_ROWS, 256)
            ):
                start = (base - names[which][0]) * 128 + which * size
                done = 0
                while done < size:
                    row, lane = divmod(start + done, 128)
                    count = min(128 - lane, size - done)
                    ref[pl.ds(done, count)] = rows[row, lane : lane + count]
                    done += count


def coordinates():
    def device(x, y, z, core):
        return (x * 4 + z // 2) * 32 + (z % 2) * 16 + y * 2 + core

    across = [
        [device(x, y, z, k) for x in range(4)]
        for z in range(8) for y in range(8) for k in range(2)
    ]
    plane = [
        [device(x, 2 * y + low, z, k) for low in range(2) for z in range(8) for y in range(4)]
        for x in range(4) for k in range(2)
    ]
    return across, plane


def reduce_owners(keep, send, scale, rest):
    mesh = ("row", "col")
    across, plane = coordinates()
    other = lax.ppermute(send, "col", [(i, i ^ 1) for i in range(32)])
    pair = (keep.astype(F32) + other.astype(F32)).astype(BF)
    got = lax.all_to_all(pair, mesh, 0, 0, axis_index_groups=across, tiled=True)
    spread, _ = pl.pallas_call(
        spread_kernel,
        out_shape=(held((640, 128)), held((8, 128), F32)),
        scratch_shapes=[pltpu.VMEM((640, 128), F32), pltpu.VMEM((656, 128), F32)],
        compiler_params=SMALL,
        name="spread",
    )(*pin(got))
    first, _ = lax.optimization_barrier((rest[0], spread))
    rest = (first, *rest[1:])
    spread = spread.reshape(64, 5, 2, 128)
    got = lax.all_to_all(spread, mesh, 0, 0, axis_index_groups=plane, tiled=True)
    got = got.reshape(640, 128)
    sums = pl.pallas_call(
        functools.partial(finish_kernel, scale),
        out_shape=tuple(jax.ShapeDtypeStruct((n,), F32) for n in (288, 576, 256)),
        scratch_shapes=[pltpu.VMEM((80, 128), F32)],
        compiler_params=SMALL,
        name="finish",
    )(*pin(got))
    return (*late(*rest), *sums)


def body(inputs, cotangent, w_conv, w_down, w_up):
    keep, send, rest = local_terms(inputs, cotangent, w_conv, w_down, w_up)
    rows, cols, _ = inputs.shape
    scale = 1.0 / math.sqrt(rows * lax.axis_size("row") * cols * lax.axis_size("col"))
    return reduce_owners(keep, send, scale, rest)


def solution(mesh):
    grid = P("row", "col", None)
    flat = P(("row", "col"))
    return jax.shard_map(
        body,
        mesh=mesh,
        in_specs=(grid, grid, P(), P(), P()),
        out_specs=(grid, grid, flat, flat, flat),
        check_vma=False,
    )
```

```python
import functools
import math

import jax
import jax.numpy as jnp
from jax import lax
from jax.experimental import pallas as pl
from jax.experimental.pallas import tpu as pltpu
from jax.sharding import PartitionSpec as P

BF = jnp.bfloat16
F32 = jnp.float32
NN = (((1,), (0,)), ((), ()))
NT = (((1,), (1,)), ((), ()))
TN = (((0,), (0,)), ((), ()))
SMALL = pltpu.CompilerParams(vmem_limit_bytes=8 * 1024 * 1024)


def held(shape, dtype=BF):
    return pltpu.VMEM(shape, dtype)


def far(*arrays):
    return tuple(pltpu.with_memory_space_constraint(a, pltpu.HBM) for a in arrays)


def pin(*arrays):
    return tuple(pltpu.with_memory_space_constraint(a, pltpu.VMEM) for a in arrays)


def swapped(odd, one, two):
    one, two = one[...].astype(F32), two[...].astype(F32)
    return jnp.where(odd, two, one), jnp.where(odd, one, two)


def mm(left, right, dims):
    return lax.dot_general(left, right, dims, preferred_element_type=F32)


def sigmoid(value):
    return 1.0 / (1.0 + jnp.exp(-value))


def weights_kernel(wc, wd, wu, conv_fwd, conv_bwd, up, down_even, down_odd):
    zero = jnp.zeros((128, 128), BF)
    for p in range(3):
        for blk in range(4):
            rows = slice(blk * 128, (blk + 1) * 128)
            conv_fwd[p, rows, 0:128] = wc[p, blk] if blk < 3 else zero
            conv_fwd[p, rows, 128:256] = wc[p, blk - 1] if blk > 0 else zero
            conv_bwd[p, 0:128, rows] = wc[p, 2 - blk] if blk < 3 else zero
            conv_bwd[p, 128:256, rows] = wc[p, 3 - blk] if blk > 0 else zero
    for p in range(2):
        for q in range(2):
            up[:, (2 * p + q) * 128 : (2 * p + q + 1) * 128] = wu[p, q]
    wide = jnp.zeros((128, 256), BF)
    down_even[0:128, 0:256] = wd[1, 1]
    down_even[0:128, 256:512] = wide
    down_even[128:256, 0:256] = wd[1, 2]
    down_even[128:256, 256:512] = wd[1, 0]
    down_odd[0:128, 0:256] = wd[2, 1]
    down_odd[0:128, 256:512] = wide
    down_odd[0:128, 512:768] = wd[0, 1]
    down_odd[0:128, 768:1024] = wide
    down_odd[128:256, 0:256] = wd[2, 2]
    down_odd[128:256, 256:512] = wd[2, 0]
    down_odd[128:256, 512:768] = wd[0, 2]
    down_odd[128:256, 768:1024] = wd[0, 0]


def prepare_weights(w_conv, w_down, w_up):
    shapes = ((3, 512, 256), (3, 256, 512), (256, 512), (256, 512), (256, 1024))
    return pl.pallas_call(
        weights_kernel,
        out_shape=tuple(held(s) for s in shapes),
        compiler_params=SMALL,
        name="weights",
    )(w_conv, w_down, w_up)


CONV_ROWS = ((0, 1, 2), (2, 3, 4), (4, 5, 6), (6, 7, 8))
DOWN_ROWS = ((0, 1, 2, 3, 4), (4, 5, 6, 7, 8), (9, 10, 11, 12, 13), (13, 14, 15, 16, 17))
UP_ROWS = ((0, 1), (2, 3), (4, 5), (6, 7))


def pack(core, ref, conv_acc, down_acc, up_acc):
    k = 0
    for owner in (core, core + 2):
        for row in CONV_ROWS[owner]:
            value = conv_acc[pl.ds(row, 128, stride=9), :]
            ref[:, 32 * k : 32 * k + 32, :] = value.reshape(4, 32, 128).astype(BF)
            k += 1
        for row in DOWN_ROWS[owner]:
            value = down_acc[row % 2, pl.ds(row // 2, 128, stride=9), :]
            ref[:, 32 * k : 32 * k + 32, :] = value.reshape(4, 32, 128).astype(BF)
            k += 1
        for row in UP_ROWS[owner]:
            value = up_acc[pl.ds(row, 128, stride=8), :]
            ref[:, 32 * k : 32 * k + 32, :] = value.reshape(4, 32, 128).astype(BF)
            k += 1


def rows_at(parts, indices):
    found = []
    for index in indices:
        for first, count, ref, place in parts:
            if first <= index < first + count:
                found.append(ref[place + index - first])
                break
    return jnp.concatenate(found, axis=0)


def x4_parts(inner, rim):
    return ((0, 4, rim, 0), (4, 32, inner, 0), (36, 4, rim, 4))


def c4_parts(inner, rim):
    return ((0, 1, rim, 0), (1, 16, inner, 0), (17, 1, rim, 1))


def f3_parts(inner, rim):
    return ((0, 4, rim, 0), (4, 30, inner, 0), (34, 4, rim, 4))


def gs_parts(inner, rim):
    return ((0, 2, rim, 0), (2, 14, inner, 0), (16, 2, rim, 2))


def own_parts(inner, rim):
    return ((0, 1, rim, 0), (1, 14, inner, 0), (15, 1, rim, 1))


def column_masks():
    at_col = lax.axis_index("col")
    half = lax.broadcasted_iota(jnp.int32, (32, 256), 0) - 2
    own = (half >= 0) & (half < 28)
    last = lax.axis_size("col") - 1
    in_grid = ((half >= 0) | (at_col != 0)) & ((half < 28) | (at_col != last))
    return jnp.where(in_grid, 1.0, 0.0), jnp.where(own, 1.0, 0.0)


def row_masks():
    at_row = lax.axis_index("row")
    last = lax.axis_size("row") - 1
    return jnp.where(at_row == 0, 0.0, 1.0), jnp.where(at_row == last, 0.0, 1.0)


def per_row(value, mask):
    count = value.shape[0] // 32
    return (value.reshape(count, 32, 256) * mask[None]).reshape(count * 32, 256)


def clear_sides(ref):
    ref[:, 0:8, :] = jnp.zeros((ref.shape[0], 8, 128), F32)
    ref[:, 64:72, :] = jnp.zeros((ref.shape[0], 8, 128), F32)


def split_x(xs, x4, places):
    for r, place in enumerate(places):
        for k in range(4):
            x4[place, :, k * 128 : (k + 1) * 128] = xs[r, pl.ds(3 + k, 32, stride=2), :].astype(BF)


def split_c(cs, c4):
    for ai in range(c4.shape[0]):
        for p in range(2):
            for q in range(2):
                k = 2 * p + q
                c4[ai, :, k * 128 : (k + 1) * 128] = cs[
                    2 * ai + p, pl.ds(4 + q, 32, stride=2), :
                ].astype(BF)


def fine_rows(x4, indices, w_fwd, in_grid):
    pre = None
    for p in range(3):
        term = mm(rows_at(x4, [i + p for i in indices]), w_fwd[p], NN)
        pre = term if pre is None else pre + term
    sig = sigmoid(pre)
    return per_row(pre * sig, in_grid), sig * (1.0 + pre * (1.0 - sig))


def store_fine(fine, slopes, f3, slope, first, count):
    behind = pltpu.roll(fine[:, 128:256], 1, 0).astype(BF).reshape(count, 32, 128)
    f3[first : first + count, :, 0:128] = behind
    f3[first : first + count, :, 128:384] = fine.astype(BF).reshape(count, 32, 256)
    slope[first : first + count] = slopes.reshape(count, 32, 256)


def coarse_rows(f3, c4, ais, w_down, w_up):
    parts = [rows_at(f3, [2 * ai + p for ai in ais]) for p in range(3)]
    cpre = mm(jnp.concatenate(parts, axis=1), w_down[...], NN)
    sig = sigmoid(cpre)
    grad = mm(rows_at(c4, ais), w_up[...], NT) * (sig * (1.0 + cpre * (1.0 - sig)))
    return cpre * sig, grad


def store_coarse(grad, gs, first, count):
    ahead = pltpu.roll(grad, count * 32 - 1, 0)
    gs[first : first + count, :, 0:256] = grad.astype(BF).reshape(count, 32, 256)
    gs[first : first + count, :, 256:512] = ahead.astype(BF).reshape(count, 32, 256)


def early_kernel(
    x, c, col_a, col_b, w_fwd, w_down, w_up,
    x4, c4, f3, slope, gs, coarse_own, g_own,
    xs, cs,
):
    left, right = swapped(lax.axis_index("col") % 2 == 1, col_b, col_a)
    for ref, own_block, first in ((xs, x, 0), (cs, c, 32)):
        clear_sides(ref)
        ref[:, 8:64, :] = own_block[...].astype(F32)
        ref[:, 4:8, :] = left[first : first + 32]
        ref[:, 64:68, :] = right[first : first + 32]
    split_x(xs, x4, range(32))
    split_c(cs, c4)
    in_grid, own = column_masks()
    for first, count in ((4, 8), (12, 8), (20, 8), (28, 6)):
        fine, slopes = fine_rows(
            x4_parts(x4, None), range(first, first + count), w_fwd, in_grid
        )
        store_fine(fine, slopes, f3, slope, first - 4, count)
    for first in (2, 9):
        coarse, grad = coarse_rows(
            f3_parts(f3, None), c4_parts(c4, None), range(first, first + 7), w_down, w_up
        )
        store_coarse(grad, gs, first - 2, 7)
        coarse_own[first - 2 : first + 5] = per_row(coarse, own).astype(BF).reshape(7, 32, 256)
        g_own[first - 2 : first + 5] = per_row(grad, own).astype(BF).reshape(7, 32, 256)


def level_kernel(
    row_a, row_b, x4_in, c4_in, f3_in, slope_in, gs_in, coarse_in, g_in,
    w_fwd, w_down, w_up, w_even, w_odd,
    keep, send, f3_rim, coarse_rim, g4,
    conv_acc, down_acc, up_acc, xs, cs, x4_rim, c4_rim, slope_rim, gs_rim, g_rim, pre_own,
):
    top, bot = swapped(lax.axis_index("row") % 2 == 1, row_b, row_a)
    for ref, at, value in (
        (xs, slice(0, 4), top[0:4]), (xs, slice(4, 7), bot[0:3]),
        (cs, slice(0, 2), top[4:6]), (cs, slice(2, 4), bot[4:6]),
    ):
        ref[at, 0:8, :] = jnp.zeros((value.shape[0], 8, 128), F32)
        ref[at, 64:72, :] = jnp.zeros((value.shape[0], 8, 128), F32)
        ref[at, 8:68, :] = value[:, 0:60]
        ref[at, 4:8, :] = value[:, 60:64]
    split_x(xs, x4_rim, range(7))
    x4_rim[7] = jnp.zeros((32, 512), BF)
    split_c(cs, c4_rim)
    in_grid, own = column_masks()
    keep_top, keep_bot = row_masks()
    x4, c4 = x4_parts(x4_in, x4_rim), c4_parts(c4_in, c4_rim)
    f3, slope = f3_parts(f3_in, f3_rim), f3_parts(slope_in, slope_rim)
    gs = gs_parts(gs_in, gs_rim)

    fine, slopes = fine_rows(x4, (0, 1, 2, 3, 34, 35, 36, 37), w_fwd, in_grid)
    fine = jnp.concatenate(
        [fine[0:96] * keep_top, fine[96:160], fine[160:256] * keep_bot], axis=0
    )
    store_fine(fine, slopes, f3_rim, slope_rim, 0, 8)

    coarse, grad = coarse_rows(f3, c4, (0, 1, 16, 17), w_down, w_up)
    store_coarse(grad, gs_rim, 0, 4)
    coarse_rim[...] = per_row(coarse[32:96], own).astype(BF).reshape(2, 32, 256)
    g_rim[...] = per_row(grad[32:96], own).astype(BF).reshape(2, 32, 256)

    coarse_flat = rows_at(own_parts(coarse_in, coarse_rim), range(16))
    res = mm(coarse_flat, rows_at(c4, range(1, 17)), TN)
    for k in range(4):
        up_acc[k * 256 : (k + 1) * 256, :] = res[:, k * 128 : (k + 1) * 128]
    g_flat = rows_at(own_parts(g_in, g_rim), range(16))
    for p in range(3):
        res = mm(rows_at(f3, [2 * a + p + 2 for a in range(16)]), g_flat, TN)
        for side in range(2):
            down_acc[side, p * 384 : (p + 1) * 384, :] = res[:, side * 128 : (side + 1) * 128]

    for first, count in ((0, 9), (9, 8)):
        ais = range(first, first + count)
        nexts = range(first + 1, first + 1 + count)
        for odd in (True, False):
            below = rows_at(gs, nexts)
            if odd:
                spread = mm(jnp.concatenate([rows_at(gs, ais), below], axis=1), w_odd[...], NT)
                cot = rows_at(c4, ais)[:, 256:512]
                at = 2
            else:
                spread = mm(below, w_even[...], NT)
                cot = rows_at(c4, nexts)[:, 0:256]
                at = 3
            slopes = rows_at(slope, [2 * ai + at for ai in ais])
            grad = per_row((cot.astype(F32) + spread) * slopes, in_grid)
            if first == 0 and odd:
                grad = jnp.concatenate([grad[0:32] * keep_top, grad[32:]], axis=0)
            if first != 0 and not odd:
                edge = (count - 1) * 32
                grad = jnp.concatenate([grad[:edge], grad[edge:] * keep_bot], axis=0)
            behind = pltpu.roll(grad[:, 128:256], 1, 0).astype(BF)
            ahead = pltpu.roll(grad[:, 0:128], count * 32 - 1, 0).astype(BF)
            rounded = grad.astype(BF)
            kept = per_row(grad, own).astype(BF)
            for ai in ais:
                g_row = 2 * ai + (0 if odd else 1)
                rows = slice((ai - first) * 32, (ai - first + 1) * 32)
                g4[g_row, :, 0:128] = behind[rows]
                g4[g_row, :, 128:384] = rounded[rows]
                g4[g_row, :, 384:512] = ahead[rows]
                if 1 <= g_row <= 32:
                    pre_own[g_row - 1] = kept[rows]

    flat = pre_own[...].reshape(1024, 256)
    for p in range(3):
        res = mm(flat, rows_at(x4, range(p + 3, p + 35)), TN)
        for q in range(3):
            tap = res[0:128, q * 128 : (q + 1) * 128] + res[128:256, (q + 1) * 128 : (q + 2) * 128]
            conv_acc[(3 * p + q) * 128 : (3 * p + q + 1) * 128, :] = tap.T

    odd_col = lax.axis_index("col") % 2 == 1

    @pl.when(jnp.logical_not(odd_col))
    def _():
        pack(0, keep, conv_acc, down_acc, up_acc)
        pack(1, send, conv_acc, down_acc, up_acc)

    @pl.when(odd_col)
    def _():
        pack(1, keep, conv_acc, down_acc, up_acc)
        pack(0, send, conv_acc, down_acc, up_acc)


def late_kernel(f3_in, f3_rim, coarse_in, coarse_rim, g4, w_up, w_bwd, out, gx, mix):
    f3 = f3_parts(f3_in, f3_rim)
    coarse = own_parts(coarse_in, coarse_rim)
    for first in (0, 8):
        up = mm(rows_at(coarse, range(first, first + 8)), w_up[...], NN)
        for a in range(first, first + 8):
            for p in range(2):
                for q in range(2):
                    k = 2 * p + q
                    value = up[(a - first) * 32 : (a - first + 1) * 32, k * 128 : (k + 1) * 128]
                    fine = rows_at(f3, [2 * a + p + 3])[:, 128 + q * 128 : 256 + q * 128]
                    value = value + fine.astype(F32)
                    mix[2 * a + p, pl.ds(4 + q, 32, stride=2), :] = value
    out[...] = mix[:, 8:64, :].astype(BF)
    for first in (0, 8, 16, 24):
        total = None
        for p in range(3):
            window = g4[first + 2 - p : first + 10 - p].reshape(256, 512)
            term = mm(window, w_bwd[p], NT)
            total = term if total is None else total + term
        for i in range(first, first + 8):
            for q in range(2):
                mix[i, pl.ds(4 + q, 32, stride=2), :] = total[
                    (i - first) * 32 : (i - first + 1) * 32, q * 128 : (q + 1) * 128
                ]
    gx[...] = mix[:, 8:64, :].astype(BF)


LARGE = pltpu.CompilerParams(vmem_limit_bytes=14 * 1024 * 1024)


def early(x, c, cols, weights, w_down):
    return pl.pallas_call(
        early_kernel,
        out_shape=(
            held((32, 32, 512)),
            held((16, 32, 512)),
            held((30, 32, 384)),
            held((30, 32, 256), F32),
            held((14, 32, 512)),
            held((14, 32, 256)),
            held((14, 32, 256)),
        ),
        scratch_shapes=[pltpu.VMEM((32, 72, 128), F32)] * 2,
        compiler_params=LARGE,
        name="early",
    )(x, c, *pin(*cols, weights[0]), w_down, *pin(weights[2]))


def level(rows, inner, weights, w_down):
    w_fwd, w_bwd, w_up, w_even, w_odd = weights
    return pl.pallas_call(
        level_kernel,
        out_shape=(
            held((4, 640, 128)),
            held((4, 640, 128)),
            held((8, 32, 384)),
            held((2, 32, 256)),
            held((34, 32, 512)),
        ),
        scratch_shapes=[
            pltpu.VMEM((1160, 128), F32),
            pltpu.VMEM((2, 1160, 128), F32),
            pltpu.VMEM((1032, 128), F32),
            pltpu.VMEM((7, 72, 128), F32),
            pltpu.VMEM((4, 72, 128), F32),
            pltpu.VMEM((8, 32, 512), BF),
            pltpu.VMEM((2, 32, 512), BF),
            pltpu.VMEM((8, 32, 256), F32),
            pltpu.VMEM((4, 32, 512), BF),
            pltpu.VMEM((2, 32, 256), BF),
            pltpu.VMEM((32, 32, 256), BF),
        ],
        compiler_params=LARGE,
        name="level",
    )(*pin(*rows, *inner, w_fwd), w_down, *pin(w_up, w_even, w_odd))


def late(*args):
    return pl.pallas_call(
        late_kernel,
        out_shape=(jax.ShapeDtypeStruct((32, 56, 128), BF),) * 2,
        scratch_shapes=[pltpu.VMEM((32, 72, 128), F32)],
        compiler_params=SMALL,
        name="late",
    )(*pin(*args))


def pairs(axis):
    count = lax.axis_size(axis)
    both = []
    for first in (0, 1):
        swaps = [(i, i + 1) for i in range(first, count - 1, 2)]
        both.append(swaps + [(b, a) for a, b in swaps])
    return both


def store_pair(odd, forward, backward, even_first, odd_first):
    even_first[...] = jnp.where(odd, backward, forward).astype(BF)
    odd_first[...] = jnp.where(odd, forward, backward).astype(BF)


def cols_kernel(x_last, x_first, c_last, c_first, col_a, col_b):
    rightward = jnp.concatenate([x_last[:, 4:8], c_last[:, 4:8]], axis=0).astype(F32)
    leftward = jnp.concatenate([x_first[:, 0:4], c_first[:, 0:4]], axis=0).astype(F32)
    store_pair(lax.axis_index("col") % 2 == 1, rightward, leftward, col_a, col_b)


def rows_kernel(x_last, x_first, c_last, c_first, col_a, col_b, row_a, row_b):
    left, right = swapped(lax.axis_index("col") % 2 == 1, col_b, col_a)

    def side(x, c, x_rows, c_rows):
        own = jnp.concatenate([x[...], c[...]], axis=0).astype(F32)
        after = jnp.concatenate([right[x_rows], right[c_rows]], axis=0)
        before = jnp.concatenate([left[x_rows], left[c_rows]], axis=0)
        return jnp.concatenate([own, after, before], axis=1)

    down = side(x_last, c_last, slice(28, 32), slice(62, 64))
    up = side(x_first, c_first, slice(0, 4), slice(32, 34))
    store_pair(lax.axis_index("row") % 2 == 1, down, up, row_a, row_b)


def row_block(count, at):
    return pl.BlockSpec((count, 56, 128), lambda i: (at, 0, 0))


def col_block(at):
    return pl.BlockSpec((32, 8, 128), lambda i: (0, at, 0))


def column_halo(x, c):
    whole = pl.BlockSpec((64, 4, 128), lambda i: (0, 0, 0))
    first, second = pl.pallas_call(
        cols_kernel,
        grid=(1,),
        out_shape=(jax.ShapeDtypeStruct((64, 4, 128), BF),) * 2,
        in_specs=[col_block(at) for at in (6, 0, 6, 0)],
        out_specs=(whole, whole),
        compiler_params=SMALL,
        name="cols",
    )(*far(x, x, c, c))
    even, odd = pairs("col")
    return lax.ppermute(first, "col", even), lax.ppermute(second, "col", odd)


def row_halo(x, c, cols):
    whole = pl.BlockSpec((6, 64, 128), lambda i: (0, 0, 0))
    first, second = pl.pallas_call(
        rows_kernel,
        grid=(1,),
        out_shape=(jax.ShapeDtypeStruct((6, 64, 128), BF),) * 2,
        in_specs=[row_block(4, 7), row_block(4, 0), row_block(2, 15), row_block(2, 0)]
        + [pl.BlockSpec((64, 4, 128), lambda i: (0, 0, 0))] * 2,
        out_specs=(whole, whole),
        compiler_params=SMALL,
        name="rows",
    )(*far(x, x, c, c), *pin(*cols))
    even, odd = pairs("row")
    return lax.ppermute(first, "row", even), lax.ppermute(second, "row", odd)


def local_terms(inputs, cotangent, w_conv, w_down, w_up):
    flat_down = w_down.reshape(1152, 256)
    weights = prepare_weights(w_conv, w_down, w_up)
    cols = column_halo(inputs, cotangent)
    rows = row_halo(inputs, cotangent, cols)
    inner = early(inputs, cotangent, cols, weights, flat_down)
    keep, send, f3_rim, coarse_rim, g4 = level(rows, inner, weights, flat_down)
    return keep, send, (inner[2], f3_rim, inner[5], coarse_rim, g4, weights[2], weights[1])


def spread_kernel(received, out, total, stage):
    total[...] = jnp.sum(received[...].astype(F32), axis=0)
    for k in range(20):
        first = (k // 10) * 320 + k % 10
        stage[pl.ds(first, 32, stride=10), :] = total[32 * k : 32 * k + 32, :]
    out[...] = stage[0:640, :].astype(BF)


def finish_kernel(scale, received, conv, down, up, stage):
    total = received[0:80, :].astype(F32)
    for chunk in range(1, 8):
        total = total + received[80 * chunk : 80 * chunk + 80, :].astype(F32)
    stage[...] = total
    rows = stage[0:10, :]
    for holder in range(1, 8):
        rows = rows + stage[10 * holder : 10 * holder + 10, :]
    rows = rows * scale
    for which in range(4):

        @pl.when(lax.axis_index("col") % 4 == which)
        def _():
            for ref, base, names, size in (
                (conv, 0, CONV_ROWS, 288), (down, 3, DOWN_ROWS, 576), (up, 8, UP_ROWS, 256)
            ):
                start = (base - names[which][0]) * 128 + which * size
                done = 0
                while done < size:
                    row, lane = divmod(start + done, 128)
                    count = min(128 - lane, size - done)
                    ref[pl.ds(done, count)] = rows[row, lane : lane + count]
                    done += count


def coordinates():
    def device(x, y, z, core):
        return (x * 4 + z // 2) * 32 + (z % 2) * 16 + y * 2 + core

    across = [
        [device(x, y, z, k) for x in range(4)]
        for z in range(8) for y in range(8) for k in range(2)
    ]
    plane = [
        [device(x, 2 * y + low, z, k) for low in range(2) for z in range(8) for y in range(4)]
        for x in range(4) for k in range(2)
    ]
    return across, plane


def reduce_owners(keep, send, scale, rest):
    mesh = ("row", "col")
    across, plane = coordinates()
    other = lax.ppermute(send, "col", [(i, i ^ 1) for i in range(32)])
    pair = (keep.astype(F32) + other.astype(F32)).astype(BF)
    got = lax.all_to_all(pair, mesh, 0, 0, axis_index_groups=across, tiled=True)
    spread = pl.pallas_call(
        spread_kernel,
        out_shape=jax.ShapeDtypeStruct((640, 128), BF),
        scratch_shapes=[pltpu.VMEM((640, 128), F32), pltpu.VMEM((656, 128), F32)],
        compiler_params=SMALL,
        name="spread",
    )(*pin(got))
    g4, _ = lax.optimization_barrier((rest[4], spread))
    rest = (*rest[:4], g4, *rest[5:])
    spread = spread.reshape(64, 5, 2, 128)
    got = lax.all_to_all(spread, mesh, 0, 0, axis_index_groups=plane, tiled=True)
    got = got.reshape(640, 128)
    sums = pl.pallas_call(
        functools.partial(finish_kernel, scale),
        out_shape=tuple(jax.ShapeDtypeStruct((n,), F32) for n in (288, 576, 256)),
        scratch_shapes=[pltpu.VMEM((80, 128), F32)],
        compiler_params=SMALL,
        name="finish",
    )(*pin(got))
    return (*late(*rest), *sums)


def body(inputs, cotangent, w_conv, w_down, w_up):
    keep, send, rest = local_terms(inputs, cotangent, w_conv, w_down, w_up)
    rows, cols, _ = inputs.shape
    scale = 1.0 / math.sqrt(rows * lax.axis_size("row") * cols * lax.axis_size("col"))
    return reduce_owners(keep, send, scale, rest)


def solution(mesh):
    grid = P("row", "col", None)
    flat = P(("row", "col"))
    return jax.shard_map(
        body,
        mesh=mesh,
        in_specs=(grid, grid, P(), P(), P()),
        out_specs=(grid, grid, flat, flat, flat),
        check_vma=False,
    )
```

```python
import functools
import math

import jax
import jax.numpy as jnp
from jax import lax
from jax.experimental import pallas as pl
from jax.experimental.pallas import tpu as pltpu
from jax.sharding import PartitionSpec as P

BF = jnp.bfloat16
F32 = jnp.float32
NN = (((1,), (0,)), ((), ()))
NT = (((1,), (1,)), ((), ()))
TN = (((0,), (0,)), ((), ()))
SMALL = pltpu.CompilerParams(vmem_limit_bytes=8 * 1024 * 1024)


def held(shape, dtype=BF):
    return pltpu.VMEM(shape, dtype)


def far(*arrays):
    return tuple(pltpu.with_memory_space_constraint(a, pltpu.HBM) for a in arrays)


def pin(*arrays):
    return tuple(pltpu.with_memory_space_constraint(a, pltpu.VMEM) for a in arrays)


def swapped(odd, one, two):
    one, two = one[...].astype(F32), two[...].astype(F32)
    return jnp.where(odd, two, one), jnp.where(odd, one, two)


def mm(left, right, dims):
    return lax.dot_general(left, right, dims, preferred_element_type=F32)


def sigmoid(value):
    return 1.0 / (1.0 + jnp.exp(-value))


def weights_kernel(wc, wd, wu, conv_fwd, conv_bwd, up, down_even, down_odd):
    zero = jnp.zeros((128, 128), BF)
    for p in range(3):
        for blk in range(4):
            rows = slice(blk * 128, (blk + 1) * 128)
            conv_fwd[p, rows, 0:128] = wc[p, blk] if blk < 3 else zero
            conv_fwd[p, rows, 128:256] = wc[p, blk - 1] if blk > 0 else zero
            conv_bwd[p, 0:128, rows] = wc[p, 2 - blk] if blk < 3 else zero
            conv_bwd[p, 128:256, rows] = wc[p, 3 - blk] if blk > 0 else zero
    for p in range(2):
        for q in range(2):
            up[:, (2 * p + q) * 128 : (2 * p + q + 1) * 128] = wu[p, q]
    wide = jnp.zeros((128, 256), BF)
    down_even[0:128, 0:256] = wd[1, 1]
    down_even[0:128, 256:512] = wide
    down_even[128:256, 0:256] = wd[1, 2]
    down_even[128:256, 256:512] = wd[1, 0]
    down_odd[0:128, 0:256] = wd[2, 1]
    down_odd[0:128, 256:512] = wide
    down_odd[0:128, 512:768] = wd[0, 1]
    down_odd[0:128, 768:1024] = wide
    down_odd[128:256, 0:256] = wd[2, 2]
    down_odd[128:256, 256:512] = wd[2, 0]
    down_odd[128:256, 512:768] = wd[0, 2]
    down_odd[128:256, 768:1024] = wd[0, 0]


def prepare_weights(w_conv, w_down, w_up):
    shapes = ((3, 512, 256), (3, 256, 512), (256, 512), (256, 512), (256, 1024))
    return pl.pallas_call(
        weights_kernel,
        out_shape=tuple(held(s) for s in shapes),
        compiler_params=SMALL,
        name="weights",
    )(w_conv, w_down, w_up)


CONV_ROWS = ((0, 1, 2), (2, 3, 4), (4, 5, 6), (6, 7, 8))
DOWN_ROWS = ((0, 1, 2, 3, 4), (4, 5, 6, 7, 8), (9, 10, 11, 12, 13), (13, 14, 15, 16, 17))
UP_ROWS = ((0, 1), (2, 3), (4, 5), (6, 7))


def pack(core, ref, conv_acc, down_acc, up_acc):
    k = 0
    for owner in (core, core + 2):
        for row in CONV_ROWS[owner]:
            value = conv_acc[pl.ds(row, 128, stride=9), :]
            ref[:, 32 * k : 32 * k + 32, :] = value.reshape(4, 32, 128).astype(BF)
            k += 1
        for row in DOWN_ROWS[owner]:
            value = down_acc[row % 2, pl.ds(row // 2, 128, stride=9), :]
            ref[:, 32 * k : 32 * k + 32, :] = value.reshape(4, 32, 128).astype(BF)
            k += 1
        for row in UP_ROWS[owner]:
            value = up_acc[pl.ds(row, 128, stride=8), :]
            ref[:, 32 * k : 32 * k + 32, :] = value.reshape(4, 32, 128).astype(BF)
            k += 1


def rows_at(parts, indices):
    found = []
    for index in indices:
        for first, count, ref, place in parts:
            if first <= index < first + count:
                found.append(ref[place + index - first])
                break
    return jnp.concatenate(found, axis=0)


def x4_parts(inner, rim):
    return ((0, 4, rim, 0), (4, 32, inner, 0), (36, 4, rim, 4))


def c4_parts(inner, rim):
    return ((0, 1, rim, 0), (1, 16, inner, 0), (17, 1, rim, 1))


def f3_parts(inner, rim):
    return ((0, 4, rim, 0), (4, 30, inner, 0), (34, 4, rim, 4))


def gs_parts(inner, rim):
    return ((0, 2, rim, 0), (2, 14, inner, 0), (16, 2, rim, 2))


def own_parts(inner, rim):
    return ((0, 1, rim, 0), (1, 14, inner, 0), (15, 1, rim, 1))


def column_masks():
    at_col = lax.axis_index("col")
    half = lax.broadcasted_iota(jnp.int32, (32, 256), 0) - 2
    own = (half >= 0) & (half < 28)
    last = lax.axis_size("col") - 1
    in_grid = ((half >= 0) | (at_col != 0)) & ((half < 28) | (at_col != last))
    return jnp.where(in_grid, 1.0, 0.0), jnp.where(own, 1.0, 0.0)


def row_masks():
    at_row = lax.axis_index("row")
    last = lax.axis_size("row") - 1
    return jnp.where(at_row == 0, 0.0, 1.0), jnp.where(at_row == last, 0.0, 1.0)


def per_row(value, mask):
    count = value.shape[0] // 32
    return (value.reshape(count, 32, 256) * mask[None]).reshape(count * 32, 256)


def clear_sides(ref):
    ref[:, 0:8, :] = jnp.zeros((ref.shape[0], 8, 128), F32)
    ref[:, 64:72, :] = jnp.zeros((ref.shape[0], 8, 128), F32)


def split_x(xs, x4, places):
    for r, place in enumerate(places):
        for k in range(4):
            x4[place, :, k * 128 : (k + 1) * 128] = xs[r, pl.ds(3 + k, 32, stride=2), :].astype(BF)


def split_c(cs, c4):
    for ai in range(c4.shape[0]):
        for p in range(2):
            for q in range(2):
                k = 2 * p + q
                c4[ai, :, k * 128 : (k + 1) * 128] = cs[
                    2 * ai + p, pl.ds(4 + q, 32, stride=2), :
                ].astype(BF)


def fine_rows(x4, indices, w_fwd, in_grid):
    pre = None
    for p in range(3):
        term = mm(rows_at(x4, [i + p for i in indices]), w_fwd[p], NN)
        pre = term if pre is None else pre + term
    sig = sigmoid(pre)
    return per_row(pre * sig, in_grid), sig * (1.0 + pre * (1.0 - sig))


def store_fine(fine, slopes, f3, slope, first, count):
    behind = pltpu.roll(fine[:, 128:256], 1, 0).astype(BF).reshape(count, 32, 128)
    f3[first : first + count, :, 0:128] = behind
    f3[first : first + count, :, 128:384] = fine.astype(BF).reshape(count, 32, 256)
    slope[first : first + count] = slopes.reshape(count, 32, 256)


def coarse_rows(f3, c4, ais, w_down, w_up):
    parts = [rows_at(f3, [2 * ai + p for ai in ais]) for p in range(3)]
    cpre = mm(jnp.concatenate(parts, axis=1), w_down[...], NN)
    sig = sigmoid(cpre)
    grad = mm(rows_at(c4, ais), w_up[...], NT) * (sig * (1.0 + cpre * (1.0 - sig)))
    return cpre * sig, grad


def store_coarse(grad, gs, first, count):
    ahead = pltpu.roll(grad, count * 32 - 1, 0)
    gs[first : first + count, :, 0:256] = grad.astype(BF).reshape(count, 32, 256)
    gs[first : first + count, :, 256:512] = ahead.astype(BF).reshape(count, 32, 256)


def grad_rows(gs, c4, slope, ais, odd, w_even, w_odd, in_grid):
    nexts = [ai + 1 for ai in ais]
    below = rows_at(gs, nexts)
    if odd:
        spread = mm(jnp.concatenate([rows_at(gs, ais), below], axis=1), w_odd[...], NT)
        cot = rows_at(c4, ais)[:, 256:512]
    else:
        spread = mm(below, w_even[...], NT)
        cot = rows_at(c4, nexts)[:, 0:256]
    slopes = rows_at(slope, [2 * ai + (2 if odd else 3) for ai in ais])
    return per_row((cot.astype(F32) + spread) * slopes, in_grid)


def store_grad(grad, own, g4, pre_own, places, own_places):
    behind = pltpu.roll(grad[:, 128:256], 1, 0).astype(BF)
    ahead = pltpu.roll(grad[:, 0:128], grad.shape[0] - 1, 0).astype(BF)
    rounded = grad.astype(BF)
    kept = per_row(grad, own).astype(BF)
    for i, (place, own_place) in enumerate(zip(places, own_places)):
        rows = slice(i * 32, i * 32 + 32)
        g4[place, :, 0:128] = behind[rows]
        g4[place, :, 128:384] = rounded[rows]
        g4[place, :, 384:512] = ahead[rows]
        if own_place is not None:
            pre_own[own_place] = kept[rows]


def conv_taps(pre, x4, rows, p):
    res = mm(pre, rows_at(x4, [i + p + 3 for i in rows]), TN)
    return [
        res[0:128, q * 128 : (q + 1) * 128] + res[128:256, (q + 1) * 128 : (q + 2) * 128]
        for q in range(3)
    ]


def g4_parts(inner, rim):
    return ((0, 3, rim, 0), (3, 27, inner, 0), (30, 4, rim, 3))


def early_kernel(
    x, c, col_b, col_a, w_fwd, w_down, w_up, w_even, w_odd,
    x4, c4, f3, slope, gs, g4, coarse_own, conv_part, up_part, down_part,
    xs, cs, g_own, pre_own,
):
    left, right = swapped(lax.axis_index("col") % 2 == 1, col_b, col_a)
    for ref, own_block, first in ((xs, x, 0), (cs, c, 32)):
        clear_sides(ref)
        ref[:, 8:64, :] = own_block[...].astype(F32)
        ref[:, 4:8, :] = left[first : first + 32]
        ref[:, 64:68, :] = right[first : first + 32]
    split_x(xs, x4, range(32))
    split_c(cs, c4)
    in_grid, own = column_masks()
    for first, count in ((4, 8), (12, 8), (20, 8), (28, 6)):
        fine, slopes = fine_rows(
            x4_parts(x4, None), range(first, first + count), w_fwd, in_grid
        )
        store_fine(fine, slopes, f3, slope, first - 4, count)
    for first in (2, 9):
        coarse, grad = coarse_rows(
            f3_parts(f3, None), c4_parts(c4, None), range(first, first + 7), w_down, w_up
        )
        store_coarse(grad, gs, first - 2, 7)
        coarse_own[first - 2 : first + 5] = per_row(coarse, own).astype(BF).reshape(7, 32, 256)
        g_own[first - 2 : first + 5] = per_row(grad, own).astype(BF).reshape(7, 32, 256)
    x4_all, c4_all, f3_all = x4_parts(x4, None), c4_parts(c4, None), f3_parts(f3, None)
    gs_all, slope_all = gs_parts(gs, None), f3_parts(slope, None)
    coarse_flat = coarse_own[...].reshape(448, 256)
    up_part[...] = mm(coarse_flat, rows_at(c4_all, range(2, 16)), TN)
    g_flat = g_own[...].reshape(448, 256)
    for p in range(3):
        window = rows_at(f3_all, [2 * a + p + 2 for a in range(1, 15)])
        down_part[p * 384 : (p + 1) * 384, :] = mm(window, g_flat, TN)
    for odd, ais in ((True, range(2, 9)), (True, range(9, 15)), (False, range(1, 8)), (False, range(8, 15))):
        grad = grad_rows(gs_all, c4_all, slope_all, ais, odd, w_even, w_odd, in_grid)
        at = [2 * ai - 3 + (0 if odd else 1) for ai in ais]
        store_grad(grad, own, g4, pre_own, at, at)
    flat = pre_own[...].reshape(864, 256)
    for p in range(3):
        for q, tap in enumerate(conv_taps(flat, x4_all, range(2, 29), p)):
            conv_part[:, (3 * p + q) * 128 : (3 * p + q + 1) * 128] = tap


def level_kernel(
    row_b, row_a, x4_in, c4_in, f3_in, slope_in, gs_in, conv_part, up_part, down_part,
    w_fwd, w_down, w_up, w_even, w_odd,
    keep, send, f3_rim, coarse_rim, g4_rim,
    conv_acc, down_acc, up_acc, xs, cs, x4_rim, c4_rim, slope_rim, gs_rim, g_rim, pre_rim,
):
    top, bot = swapped(lax.axis_index("row") % 2 == 1, row_b, row_a)
    for ref, at, value in (
        (xs, slice(0, 4), top[0:4]), (xs, slice(4, 7), bot[0:3]),
        (cs, slice(0, 2), top[4:6]), (cs, slice(2, 4), bot[4:6]),
    ):
        ref[at, 0:8, :] = jnp.zeros((value.shape[0], 8, 128), F32)
        ref[at, 64:72, :] = jnp.zeros((value.shape[0], 8, 128), F32)
        ref[at, 8:68, :] = value[:, 0:60]
        ref[at, 4:8, :] = value[:, 60:64]
    split_x(xs, x4_rim, range(7))
    x4_rim[7] = jnp.zeros((32, 512), BF)
    split_c(cs, c4_rim)
    in_grid, own = column_masks()
    keep_top, keep_bot = row_masks()
    x4, c4 = x4_parts(x4_in, x4_rim), c4_parts(c4_in, c4_rim)
    f3, slope = f3_parts(f3_in, f3_rim), f3_parts(slope_in, slope_rim)
    gs = gs_parts(gs_in, gs_rim)

    fine, slopes = fine_rows(x4, (0, 1, 2, 3, 34, 35, 36, 37), w_fwd, in_grid)
    fine = jnp.concatenate(
        [fine[0:96] * keep_top, fine[96:160], fine[160:256] * keep_bot], axis=0
    )
    store_fine(fine, slopes, f3_rim, slope_rim, 0, 8)

    coarse, grad = coarse_rows(f3, c4, (0, 1, 16, 17), w_down, w_up)
    store_coarse(grad, gs_rim, 0, 4)
    coarse_rim[...] = per_row(coarse[32:96], own).astype(BF).reshape(2, 32, 256)
    g_rim[...] = per_row(grad[32:96], own).astype(BF).reshape(2, 32, 256)

    res = up_part[...] + mm(coarse_rim[...].reshape(64, 256), rows_at(c4, (1, 16)), TN)
    for k in range(4):
        up_acc[k * 256 : (k + 1) * 256, :] = res[:, k * 128 : (k + 1) * 128]
    g_flat = g_rim[...].reshape(64, 256)
    for p in range(3):
        at = slice(p * 384, (p + 1) * 384)
        res = down_part[at, :] + mm(rows_at(f3, (p + 2, p + 32)), g_flat, TN)
        for side in range(2):
            down_acc[side, at, :] = res[:, side * 128 : (side + 1) * 128]

    grad = grad_rows(gs, c4, slope, (0, 1, 15, 16), True, w_even, w_odd, in_grid)
    grad = jnp.concatenate([grad[0:32] * keep_top, grad[32:]], axis=0)
    store_grad(grad, own, g4_rim, pre_rim, (0, 2, 3, 5), (None, 1, 2, 4))
    grad = grad_rows(gs, c4, slope, (0, 15, 16), False, w_even, w_odd, in_grid)
    grad = jnp.concatenate([grad[0:64], grad[64:] * keep_bot], axis=0)
    store_grad(grad, own, g4_rim, pre_rim, (1, 4, 6), (0, 3, None))

    flat = pre_rim[...].reshape(160, 256)
    for p in range(3):
        for q, tap in enumerate(conv_taps(flat, x4, (0, 1, 29, 30, 31), p)):
            at = slice((3 * p + q) * 128, (3 * p + q + 1) * 128)
            conv_acc[at, :] = (conv_part[:, at] + tap).T

    odd_col = lax.axis_index("col") % 2 == 1

    @pl.when(jnp.logical_not(odd_col))
    def _():
        pack(0, keep, conv_acc, down_acc, up_acc)
        pack(1, send, conv_acc, down_acc, up_acc)

    @pl.when(odd_col)
    def _():
        pack(1, keep, conv_acc, down_acc, up_acc)
        pack(0, send, conv_acc, down_acc, up_acc)


def late_kernel(
    f3_in, f3_rim, coarse_in, coarse_rim, g4_in, g4_rim, w_up, w_bwd, out, gx, mix
):
    g4 = g4_parts(g4_in, g4_rim)
    f3 = f3_parts(f3_in, f3_rim)
    coarse = own_parts(coarse_in, coarse_rim)
    for first in (0, 8):
        up = mm(rows_at(coarse, range(first, first + 8)), w_up[...], NN)
        for a in range(first, first + 8):
            for p in range(2):
                for q in range(2):
                    k = 2 * p + q
                    value = up[(a - first) * 32 : (a - first + 1) * 32, k * 128 : (k + 1) * 128]
                    fine = rows_at(f3, [2 * a + p + 3])[:, 128 + q * 128 : 256 + q * 128]
                    value = value + fine.astype(F32)
                    mix[2 * a + p, pl.ds(4 + q, 32, stride=2), :] = value
    out[...] = mix[:, 8:64, :].astype(BF)
    for first in (0, 8, 16, 24):
        total = None
        for p in range(3):
            window = rows_at(g4, range(first + 2 - p, first + 10 - p))
            term = mm(window, w_bwd[p], NT)
            total = term if total is None else total + term
        for i in range(first, first + 8):
            for q in range(2):
                mix[i, pl.ds(4 + q, 32, stride=2), :] = total[
                    (i - first) * 32 : (i - first + 1) * 32, q * 128 : (q + 1) * 128
                ]
    gx[...] = mix[:, 8:64, :].astype(BF)


LARGE = pltpu.CompilerParams(vmem_limit_bytes=16 * 1024 * 1024)


def early(x, c, cols, weights, w_down):
    return pl.pallas_call(
        early_kernel,
        out_shape=(
            held((32, 32, 512)),
            held((16, 32, 512)),
            held((30, 32, 384)),
            held((30, 32, 256), F32),
            held((14, 32, 512)),
            held((27, 32, 512)),
            held((14, 32, 256)),
            held((128, 1152), F32),
            held((256, 512), F32),
            held((1152, 256), F32),
        ),
        scratch_shapes=[pltpu.VMEM((32, 72, 128), F32)] * 2
        + [pltpu.VMEM((14, 32, 256), BF), pltpu.VMEM((27, 32, 256), BF)],
        compiler_params=LARGE,
        name="early",
    )(x, c, *pin(*cols, weights[0]), w_down, *pin(*weights[2:]))


def level(rows, inner, weights, w_down):
    w_fwd, w_bwd, w_up, w_even, w_odd = weights
    return pl.pallas_call(
        level_kernel,
        out_shape=(
            held((4, 640, 128)),
            held((4, 640, 128)),
            held((8, 32, 384)),
            held((2, 32, 256)),
            held((7, 32, 512)),
        ),
        scratch_shapes=[
            pltpu.VMEM((1160, 128), F32),
            pltpu.VMEM((2, 1160, 128), F32),
            pltpu.VMEM((1032, 128), F32),
            pltpu.VMEM((7, 72, 128), F32),
            pltpu.VMEM((4, 72, 128), F32),
            pltpu.VMEM((8, 32, 512), BF),
            pltpu.VMEM((2, 32, 512), BF),
            pltpu.VMEM((8, 32, 256), F32),
            pltpu.VMEM((4, 32, 512), BF),
            pltpu.VMEM((2, 32, 256), BF),
            pltpu.VMEM((5, 32, 256), BF),
        ],
        compiler_params=LARGE,
        name="level",
    )(*pin(*rows, *inner[:5], *inner[7:], w_fwd), w_down, *pin(w_up, w_even, w_odd))


def late(*args):
    return pl.pallas_call(
        late_kernel,
        out_shape=(jax.ShapeDtypeStruct((32, 56, 128), BF),) * 2,
        scratch_shapes=[pltpu.VMEM((32, 72, 128), F32)],
        compiler_params=SMALL,
        name="late",
    )(*pin(*args))


def pairs(axis):
    count = lax.axis_size(axis)
    both = []
    for first in (0, 1):
        swaps = [(i, i + 1) for i in range(first, count - 1, 2)]
        both.append(swaps + [(b, a) for a, b in swaps])
    return both


def swap(longer, shorter, axis):
    even, odd = pairs(axis)
    return lax.ppermute(longer, axis, odd), lax.ppermute(shorter, axis, even)


def store_pair(odd, forward, backward, even_first, odd_first):
    even_first[...] = jnp.where(odd, backward, forward).astype(BF)
    odd_first[...] = jnp.where(odd, forward, backward).astype(BF)


def cols_kernel(x_last, x_first, c_last, c_first, col_b, col_a):
    rightward = jnp.concatenate([x_last[:, 4:8], c_last[:, 4:8]], axis=0).astype(F32)
    leftward = jnp.concatenate([x_first[:, 0:4], c_first[:, 0:4]], axis=0).astype(F32)
    store_pair(lax.axis_index("col") % 2 == 1, rightward, leftward, col_a, col_b)


def rows_kernel(x_last, x_first, c_last, c_first, col_b, col_a, row_b, row_a):
    left, right = swapped(lax.axis_index("col") % 2 == 1, col_b, col_a)

    def side(x, c, x_rows, c_rows):
        own = jnp.concatenate([x[...], c[...]], axis=0).astype(F32)
        after = jnp.concatenate([right[x_rows], right[c_rows]], axis=0)
        before = jnp.concatenate([left[x_rows], left[c_rows]], axis=0)
        return jnp.concatenate([own, after, before], axis=1)

    down = side(x_last, c_last, slice(28, 32), slice(62, 64))
    up = side(x_first, c_first, slice(0, 4), slice(32, 34))
    store_pair(lax.axis_index("row") % 2 == 1, down, up, row_a, row_b)


def row_block(count, at):
    return pl.BlockSpec((count, 56, 128), lambda i: (at, 0, 0))


def col_block(at):
    return pl.BlockSpec((32, 8, 128), lambda i: (0, at, 0))


def column_halo(x, c):
    whole = pl.BlockSpec((64, 4, 128), lambda i: (0, 0, 0))
    first, second = pl.pallas_call(
        cols_kernel,
        grid=(1,),
        out_shape=(jax.ShapeDtypeStruct((64, 4, 128), BF),) * 2,
        in_specs=[col_block(at) for at in (6, 0, 6, 0)],
        out_specs=(whole, whole),
        compiler_params=SMALL,
        name="cols",
    )(*far(x, x, c, c))
    return swap(first, second, "col")


def row_halo(x, c, cols):
    whole = pl.BlockSpec((6, 64, 128), lambda i: (0, 0, 0))
    first, second = pl.pallas_call(
        rows_kernel,
        grid=(1,),
        out_shape=(jax.ShapeDtypeStruct((6, 64, 128), BF),) * 2,
        in_specs=[row_block(4, 7), row_block(4, 0), row_block(2, 15), row_block(2, 0)]
        + [pl.BlockSpec((64, 4, 128), lambda i: (0, 0, 0))] * 2,
        out_specs=(whole, whole),
        compiler_params=SMALL,
        name="rows",
    )(*far(x, x, c, c), *pin(*cols))
    return swap(first, second, "row")


def local_terms(inputs, cotangent, w_conv, w_down, w_up):
    flat_down = w_down.reshape(1152, 256)
    weights = prepare_weights(w_conv, w_down, w_up)
    cols = column_halo(inputs, cotangent)
    rows = row_halo(inputs, cotangent, cols)
    inner = early(inputs, cotangent, cols, weights, flat_down)
    keep, send, f3_rim, coarse_rim, g4_rim = level(rows, inner, weights, flat_down)
    held_back = (inner[2], f3_rim, inner[6], coarse_rim, inner[5], g4_rim, weights[2], weights[1])
    return keep, send, held_back


def spread_kernel(received, out, total, stage):
    total[...] = jnp.sum(received[...].astype(F32), axis=0)
    for k in range(20):
        first = (k // 10) * 320 + k % 10
        stage[pl.ds(first, 32, stride=10), :] = total[32 * k : 32 * k + 32, :]
    out[...] = stage[0:640, :].astype(BF)


def finish_kernel(scale, received, conv, down, up, stage):
    total = received[0:80, :].astype(F32)
    for chunk in range(1, 8):
        total = total + received[80 * chunk : 80 * chunk + 80, :].astype(F32)
    stage[...] = total
    rows = stage[0:10, :]
    for holder in range(1, 8):
        rows = rows + stage[10 * holder : 10 * holder + 10, :]
    rows = rows * scale
    for which in range(4):

        @pl.when(lax.axis_index("col") % 4 == which)
        def _():
            for ref, base, names, size in (
                (conv, 0, CONV_ROWS, 288), (down, 3, DOWN_ROWS, 576), (up, 8, UP_ROWS, 256)
            ):
                start = (base - names[which][0]) * 128 + which * size
                done = 0
                while done < size:
                    row, lane = divmod(start + done, 128)
                    count = min(128 - lane, size - done)
                    ref[pl.ds(done, count)] = rows[row, lane : lane + count]
                    done += count


def coordinates():
    def device(x, y, z, core):
        return (x * 4 + z // 2) * 32 + (z % 2) * 16 + y * 2 + core

    across = [
        [device(x, y, z, k) for x in range(4)]
        for z in range(8) for y in range(8) for k in range(2)
    ]
    plane = [
        [device(x, 2 * y + low, z, k) for low in range(2) for z in range(8) for y in range(4)]
        for x in range(4) for k in range(2)
    ]
    return across, plane


def reduce_owners(keep, send, scale, rest):
    mesh = ("row", "col")
    across, plane = coordinates()
    other = lax.ppermute(send, "col", [(i, i ^ 1) for i in range(32)])
    pair = (keep.astype(F32) + other.astype(F32)).astype(BF)
    got = lax.all_to_all(pair, mesh, 0, 0, axis_index_groups=across, tiled=True)
    spread = pl.pallas_call(
        spread_kernel,
        out_shape=jax.ShapeDtypeStruct((640, 128), BF),
        scratch_shapes=[pltpu.VMEM((640, 128), F32), pltpu.VMEM((656, 128), F32)],
        compiler_params=SMALL,
        name="spread",
    )(*pin(got))
    rim, _ = lax.optimization_barrier((rest[5], spread))
    rest = (*rest[:5], rim, *rest[6:])
    spread = spread.reshape(64, 5, 2, 128)
    got = lax.all_to_all(spread, mesh, 0, 0, axis_index_groups=plane, tiled=True)
    got = got.reshape(640, 128)
    sums = pl.pallas_call(
        functools.partial(finish_kernel, scale),
        out_shape=tuple(jax.ShapeDtypeStruct((n,), F32) for n in (288, 576, 256)),
        scratch_shapes=[pltpu.VMEM((80, 128), F32)],
        compiler_params=SMALL,
        name="finish",
    )(*pin(got))
    return (*late(*rest), *sums)


def body(inputs, cotangent, w_conv, w_down, w_up):
    keep, send, rest = local_terms(inputs, cotangent, w_conv, w_down, w_up)
    rows, cols, _ = inputs.shape
    scale = 1.0 / math.sqrt(rows * lax.axis_size("row") * cols * lax.axis_size("col"))
    return reduce_owners(keep, send, scale, rest)


def solution(mesh):
    grid = P("row", "col", None)
    flat = P(("row", "col"))
    return jax.shard_map(
        body,
        mesh=mesh,
        in_specs=(grid, grid, P(), P(), P()),
        out_specs=(grid, grid, flat, flat, flat),
        check_vma=False,
    )
```

```python
import functools
import math

import jax
import jax.numpy as jnp
from jax import lax
from jax.experimental import pallas as pl
from jax.experimental.pallas import tpu as pltpu
from jax.sharding import PartitionSpec as P

BF = jnp.bfloat16
F32 = jnp.float32
NN = (((1,), (0,)), ((), ()))
NT = (((1,), (1,)), ((), ()))
TN = (((0,), (0,)), ((), ()))
SMALL = pltpu.CompilerParams(vmem_limit_bytes=8 * 1024 * 1024)


def held(shape, dtype=BF):
    return pltpu.VMEM(shape, dtype)


def far(*arrays):
    return tuple(pltpu.with_memory_space_constraint(a, pltpu.HBM) for a in arrays)


def pin(*arrays):
    return tuple(pltpu.with_memory_space_constraint(a, pltpu.VMEM) for a in arrays)


def swapped(odd, one, two):
    one, two = one[...].astype(F32), two[...].astype(F32)
    return jnp.where(odd, two, one), jnp.where(odd, one, two)


def mm(left, right, dims):
    return lax.dot_general(left, right, dims, preferred_element_type=F32)


def sigmoid(value):
    return 1.0 / (1.0 + jnp.exp(-value))


def weights_kernel(wc, wd, wu, conv_fwd, conv_bwd, up, down_even, down_odd):
    zero = jnp.zeros((128, 128), BF)
    for p in range(3):
        for blk in range(4):
            rows = slice(blk * 128, (blk + 1) * 128)
            conv_fwd[p, rows, 0:128] = wc[p, blk] if blk < 3 else zero
            conv_fwd[p, rows, 128:256] = wc[p, blk - 1] if blk > 0 else zero
            conv_bwd[p, 0:128, rows] = wc[p, 2 - blk] if blk < 3 else zero
            conv_bwd[p, 128:256, rows] = wc[p, 3 - blk] if blk > 0 else zero
    for p in range(2):
        for q in range(2):
            up[:, (2 * p + q) * 128 : (2 * p + q + 1) * 128] = wu[p, q]
    wide = jnp.zeros((128, 256), BF)
    down_even[0:128, 0:256] = wd[1, 1]
    down_even[0:128, 256:512] = wide
    down_even[128:256, 0:256] = wd[1, 2]
    down_even[128:256, 256:512] = wd[1, 0]
    down_odd[0:128, 0:256] = wd[2, 1]
    down_odd[0:128, 256:512] = wide
    down_odd[0:128, 512:768] = wd[0, 1]
    down_odd[0:128, 768:1024] = wide
    down_odd[128:256, 0:256] = wd[2, 2]
    down_odd[128:256, 256:512] = wd[2, 0]
    down_odd[128:256, 512:768] = wd[0, 2]
    down_odd[128:256, 768:1024] = wd[0, 0]


def prepare_weights(w_conv, w_down, w_up):
    shapes = ((3, 512, 256), (3, 256, 512), (256, 512), (256, 512), (256, 1024))
    return pl.pallas_call(
        weights_kernel,
        out_shape=tuple(held(s) for s in shapes),
        compiler_params=SMALL,
        name="weights",
    )(w_conv, w_down, w_up)


CONV_ROWS = ((0, 1, 2), (2, 3, 4), (4, 5, 6), (6, 7, 8))
DOWN_ROWS = ((0, 1, 2, 3, 4), (4, 5, 6, 7, 8), (9, 10, 11, 12, 13), (13, 14, 15, 16, 17))
UP_ROWS = ((0, 1), (2, 3), (4, 5), (6, 7))


def pack(core, ref, conv_acc, down_acc, up_acc):
    k = 0
    for owner in (core, core + 2):
        for row in CONV_ROWS[owner]:
            value = conv_acc[pl.ds(row, 128, stride=9), :]
            ref[:, 32 * k : 32 * k + 32, :] = value.reshape(4, 32, 128).astype(BF)
            k += 1
        for row in DOWN_ROWS[owner]:
            value = down_acc[row % 2, pl.ds(row // 2, 128, stride=9), :]
            ref[:, 32 * k : 32 * k + 32, :] = value.reshape(4, 32, 128).astype(BF)
            k += 1
        for row in UP_ROWS[owner]:
            value = up_acc[pl.ds(row, 128, stride=8), :]
            ref[:, 32 * k : 32 * k + 32, :] = value.reshape(4, 32, 128).astype(BF)
            k += 1


def rows_at(parts, indices):
    found = []
    for index in indices:
        for first, count, ref, place in parts:
            if first <= index < first + count:
                found.append(ref[place + index - first])
                break
    return jnp.concatenate(found, axis=0)


def x4_parts(inner, rim):
    return ((0, 4, rim, 0), (4, 32, inner, 0), (36, 4, rim, 4))


def c4_parts(inner, rim):
    return ((0, 1, rim, 0), (1, 16, inner, 0), (17, 1, rim, 1))


def f3_parts(inner, rim):
    return ((0, 4, rim, 0), (4, 30, inner, 0), (34, 4, rim, 4))


def gs_parts(inner, rim):
    return ((0, 2, rim, 0), (2, 14, inner, 0), (16, 2, rim, 2))


def own_parts(inner, rim):
    return ((0, 1, rim, 0), (1, 14, inner, 0), (15, 1, rim, 1))


def column_masks():
    at_col = lax.axis_index("col")
    half = lax.broadcasted_iota(jnp.int32, (32, 256), 0) - 2
    own = (half >= 0) & (half < 28)
    last = lax.axis_size("col") - 1
    in_grid = ((half >= 0) | (at_col != 0)) & ((half < 28) | (at_col != last))
    return jnp.where(in_grid, 1.0, 0.0), jnp.where(own, 1.0, 0.0)


def row_masks():
    at_row = lax.axis_index("row")
    last = lax.axis_size("row") - 1
    return jnp.where(at_row == 0, 0.0, 1.0), jnp.where(at_row == last, 0.0, 1.0)


def per_row(value, mask):
    count = value.shape[0] // 32
    return (value.reshape(count, 32, 256) * mask[None]).reshape(count * 32, 256)


def clear_sides(ref):
    ref[:, 0:8, :] = jnp.zeros((ref.shape[0], 8, 128), F32)
    ref[:, 64:72, :] = jnp.zeros((ref.shape[0], 8, 128), F32)


def split_x(xs, x4, places):
    for r, place in enumerate(places):
        for k in range(4):
            x4[place, :, k * 128 : (k + 1) * 128] = xs[r, pl.ds(3 + k, 32, stride=2), :].astype(BF)


def split_c(cs, c4):
    for ai in range(c4.shape[0]):
        for p in range(2):
            for q in range(2):
                k = 2 * p + q
                c4[ai, :, k * 128 : (k + 1) * 128] = cs[
                    2 * ai + p, pl.ds(4 + q, 32, stride=2), :
                ].astype(BF)


def fine_rows(x4, indices, w_fwd, in_grid):
    pre = None
    for p in range(3):
        term = mm(rows_at(x4, [i + p for i in indices]), w_fwd[p], NN)
        pre = term if pre is None else pre + term
    sig = sigmoid(pre)
    return per_row(pre * sig, in_grid), sig * (1.0 + pre * (1.0 - sig))


def store_fine(fine, slopes, f3, slope, first, count):
    behind = pltpu.roll(fine[:, 128:256], 1, 0).astype(BF).reshape(count, 32, 128)
    f3[first : first + count, :, 0:128] = behind
    f3[first : first + count, :, 128:384] = fine.astype(BF).reshape(count, 32, 256)
    slope[first : first + count] = slopes.reshape(count, 32, 256)


def coarse_rows(f3, c4, ais, w_down, w_up):
    parts = [rows_at(f3, [2 * ai + p for ai in ais]) for p in range(3)]
    cpre = mm(jnp.concatenate(parts, axis=1), w_down[...], NN)
    sig = sigmoid(cpre)
    grad = mm(rows_at(c4, ais), w_up[...], NT) * (sig * (1.0 + cpre * (1.0 - sig)))
    return cpre * sig, grad


def store_coarse(grad, gs, first, count):
    ahead = pltpu.roll(grad, count * 32 - 1, 0)
    gs[first : first + count, :, 0:256] = grad.astype(BF).reshape(count, 32, 256)
    gs[first : first + count, :, 256:512] = ahead.astype(BF).reshape(count, 32, 256)


def grad_rows(gs, c4, slope, ais, odd, w_even, w_odd, in_grid):
    nexts = [ai + 1 for ai in ais]
    below = rows_at(gs, nexts)
    if odd:
        spread = mm(jnp.concatenate([rows_at(gs, ais), below], axis=1), w_odd[...], NT)
        cot = rows_at(c4, ais)[:, 256:512]
    else:
        spread = mm(below, w_even[...], NT)
        cot = rows_at(c4, nexts)[:, 0:256]
    slopes = rows_at(slope, [2 * ai + (2 if odd else 3) for ai in ais])
    return per_row((cot.astype(F32) + spread) * slopes, in_grid)


def store_grad(grad, own, g4, pre_own, places, own_places):
    behind = pltpu.roll(grad[:, 128:256], 1, 0).astype(BF)
    ahead = pltpu.roll(grad[:, 0:128], grad.shape[0] - 1, 0).astype(BF)
    rounded = grad.astype(BF)
    kept = per_row(grad, own).astype(BF)
    for i, (place, own_place) in enumerate(zip(places, own_places)):
        rows = slice(i * 32, i * 32 + 32)
        g4[place, :, 0:128] = behind[rows]
        g4[place, :, 128:384] = rounded[rows]
        g4[place, :, 384:512] = ahead[rows]
        if own_place is not None:
            pre_own[own_place] = kept[rows]


def conv_taps(pre, x4, rows, p, flip):
    window = rows_at(x4, [i + p + 3 for i in rows])
    taps = []
    if flip:
        res = mm(window, pre, TN)
        for q in range(3):
            one, two = slice(q * 128, q * 128 + 128), slice(q * 128 + 128, q * 128 + 256)
            taps.append(res[one, 0:128] + res[two, 128:256])
    else:
        res = mm(pre, window, TN)
        for q in range(3):
            one, two = slice(q * 128, q * 128 + 128), slice(q * 128 + 128, q * 128 + 256)
            taps.append((res[0:128, one] + res[128:256, two]).T)
    return taps


def g4_parts(inner, rim):
    return ((0, 3, rim, 0), (3, 27, inner, 0), (30, 4, rim, 3))


def early_kernel(
    x, c, col_b, col_a, w_fwd, w_down, w_up, w_even, w_odd,
    x4, c4, f3, slope, gs, g4, coarse_own, conv_part, up_part, down_part,
    xs, cs, g_own, pre_own,
):
    left, right = swapped(lax.axis_index("col") % 2 == 1, col_b, col_a)
    for ref, own_block, first in ((xs, x, 0), (cs, c, 32)):
        clear_sides(ref)
        ref[:, 8:64, :] = own_block[...].astype(F32)
        ref[:, 4:8, :] = left[first : first + 32]
        ref[:, 64:68, :] = right[first : first + 32]
    split_x(xs, x4, range(32))
    split_c(cs, c4)
    in_grid, own = column_masks()
    for first, count in ((4, 8), (12, 8), (20, 8), (28, 6)):
        fine, slopes = fine_rows(
            x4_parts(x4, None), range(first, first + count), w_fwd, in_grid
        )
        store_fine(fine, slopes, f3, slope, first - 4, count)
    for first in (2, 9):
        coarse, grad = coarse_rows(
            f3_parts(f3, None), c4_parts(c4, None), range(first, first + 7), w_down, w_up
        )
        store_coarse(grad, gs, first - 2, 7)
        coarse_own[first - 2 : first + 5] = per_row(coarse, own).astype(BF).reshape(7, 32, 256)
        g_own[first - 2 : first + 5] = per_row(grad, own).astype(BF).reshape(7, 32, 256)
    x4_all, c4_all, f3_all = x4_parts(x4, None), c4_parts(c4, None), f3_parts(f3, None)
    gs_all, slope_all = gs_parts(gs, None), f3_parts(slope, None)
    coarse_flat = coarse_own[...].reshape(448, 256)
    up_part[...] = mm(coarse_flat, rows_at(c4_all, range(2, 16)), TN)
    g_flat = g_own[...].reshape(448, 256)
    for p in range(3):
        window = rows_at(f3_all, [2 * a + p + 2 for a in range(1, 15)])
        down_part[p * 384 : (p + 1) * 384, :] = mm(window, g_flat, TN)
    for odd, ais in ((True, range(2, 9)), (True, range(9, 15)), (False, range(1, 8)), (False, range(8, 15))):
        grad = grad_rows(gs_all, c4_all, slope_all, ais, odd, w_even, w_odd, in_grid)
        at = [2 * ai - 3 + (0 if odd else 1) for ai in ais]
        store_grad(grad, own, g4, pre_own, at, at)
    flat = pre_own[...].reshape(864, 256)
    for p in range(3):
        for q, tap in enumerate(conv_taps(flat, x4_all, range(2, 29), p, False)):
            conv_part[(3 * p + q) * 128 : (3 * p + q + 1) * 128, :] = tap


def level_kernel(
    row_b, row_a, x4_in, c4_in, f3_in, slope_in, gs_in, conv_part, up_part, down_part,
    w_fwd, w_down, w_up, w_even, w_odd,
    keep, send, f3_rim, coarse_rim, g4_rim,
    conv_acc, down_acc, up_acc, xs, cs, x4_rim, c4_rim, slope_rim, gs_rim, g_rim, pre_rim,
):
    top, bot = swapped(lax.axis_index("row") % 2 == 1, row_b, row_a)
    for ref, at, value in (
        (xs, slice(0, 4), top[0:4]), (xs, slice(4, 7), bot[0:3]),
        (cs, slice(0, 2), top[4:6]), (cs, slice(2, 4), bot[4:6]),
    ):
        ref[at, 0:8, :] = jnp.zeros((value.shape[0], 8, 128), F32)
        ref[at, 64:72, :] = jnp.zeros((value.shape[0], 8, 128), F32)
        ref[at, 8:68, :] = value[:, 0:60]
        ref[at, 4:8, :] = value[:, 60:64]
    split_x(xs, x4_rim, range(7))
    x4_rim[7] = jnp.zeros((32, 512), BF)
    split_c(cs, c4_rim)
    in_grid, own = column_masks()
    keep_top, keep_bot = row_masks()
    x4, c4 = x4_parts(x4_in, x4_rim), c4_parts(c4_in, c4_rim)
    f3, slope = f3_parts(f3_in, f3_rim), f3_parts(slope_in, slope_rim)
    gs = gs_parts(gs_in, gs_rim)

    fine, slopes = fine_rows(x4, (0, 1, 2, 3, 34, 35, 36, 37), w_fwd, in_grid)
    fine = jnp.concatenate(
        [fine[0:96] * keep_top, fine[96:160], fine[160:256] * keep_bot], axis=0
    )
    store_fine(fine, slopes, f3_rim, slope_rim, 0, 8)

    coarse, grad = coarse_rows(f3, c4, (0, 1, 16, 17), w_down, w_up)
    store_coarse(grad, gs_rim, 0, 4)
    coarse_rim[...] = per_row(coarse[32:96], own).astype(BF).reshape(2, 32, 256)
    g_rim[...] = per_row(grad[32:96], own).astype(BF).reshape(2, 32, 256)

    res = up_part[...] + mm(coarse_rim[...].reshape(64, 256), rows_at(c4, (1, 16)), TN)
    for k in range(4):
        up_acc[k * 256 : (k + 1) * 256, :] = res[:, k * 128 : (k + 1) * 128]
    g_flat = g_rim[...].reshape(64, 256)
    for p in range(3):
        at = slice(p * 384, (p + 1) * 384)
        res = down_part[at, :] + mm(rows_at(f3, (p + 2, p + 32)), g_flat, TN)
        for side in range(2):
            down_acc[side, at, :] = res[:, side * 128 : (side + 1) * 128]

    grad = grad_rows(gs, c4, slope, (0, 1, 15, 16), True, w_even, w_odd, in_grid)
    grad = jnp.concatenate([grad[0:32] * keep_top, grad[32:]], axis=0)
    store_grad(grad, own, g4_rim, pre_rim, (0, 2, 3, 5), (None, 1, 2, 4))
    grad = grad_rows(gs, c4, slope, (0, 15, 16), False, w_even, w_odd, in_grid)
    grad = jnp.concatenate([grad[0:64], grad[64:] * keep_bot], axis=0)
    store_grad(grad, own, g4_rim, pre_rim, (1, 4, 6), (0, 3, None))

    flat = pre_rim[...].reshape(160, 256)
    for p in range(3):
        for q, tap in enumerate(conv_taps(flat, x4, (0, 1, 29, 30, 31), p, True)):
            at = slice((3 * p + q) * 128, (3 * p + q + 1) * 128)
            conv_acc[at, :] = conv_part[at, :] + tap

    odd_col = lax.axis_index("col") % 2 == 1

    @pl.when(jnp.logical_not(odd_col))
    def _():
        pack(0, keep, conv_acc, down_acc, up_acc)
        pack(1, send, conv_acc, down_acc, up_acc)

    @pl.when(odd_col)
    def _():
        pack(1, keep, conv_acc, down_acc, up_acc)
        pack(0, send, conv_acc, down_acc, up_acc)


def late_kernel(
    f3_in, f3_rim, coarse_in, coarse_rim, g4_in, g4_rim, w_up, w_bwd, out, gx, mix
):
    g4 = g4_parts(g4_in, g4_rim)
    f3 = f3_parts(f3_in, f3_rim)
    coarse = own_parts(coarse_in, coarse_rim)
    for first in (0, 8):
        up = mm(rows_at(coarse, range(first, first + 8)), w_up[...], NN)
        for a in range(first, first + 8):
            for p in range(2):
                for q in range(2):
                    k = 2 * p + q
                    value = up[(a - first) * 32 : (a - first + 1) * 32, k * 128 : (k + 1) * 128]
                    fine = rows_at(f3, [2 * a + p + 3])[:, 128 + q * 128 : 256 + q * 128]
                    value = value + fine.astype(F32)
                    mix[2 * a + p, pl.ds(4 + q, 32, stride=2), :] = value
    out[...] = mix[:, 8:64, :].astype(BF)
    for first in (0, 8, 16, 24):
        total = None
        for p in range(3):
            window = rows_at(g4, range(first + 2 - p, first + 10 - p))
            term = mm(window, w_bwd[p], NT)
            total = term if total is None else total + term
        for i in range(first, first + 8):
            for q in range(2):
                mix[i, pl.ds(4 + q, 32, stride=2), :] = total[
                    (i - first) * 32 : (i - first + 1) * 32, q * 128 : (q + 1) * 128
                ]
    gx[...] = mix[:, 8:64, :].astype(BF)


LARGE = pltpu.CompilerParams(vmem_limit_bytes=16 * 1024 * 1024)


def early(x, c, cols, weights, w_down):
    return pl.pallas_call(
        early_kernel,
        out_shape=(
            held((32, 32, 512)),
            held((16, 32, 512)),
            held((30, 32, 384)),
            held((30, 32, 256), F32),
            held((14, 32, 512)),
            held((27, 32, 512)),
            held((14, 32, 256)),
            held((1152, 128), F32),
            held((256, 512), F32),
            held((1152, 256), F32),
        ),
        scratch_shapes=[pltpu.VMEM((32, 72, 128), F32)] * 2
        + [pltpu.VMEM((14, 32, 256), BF), pltpu.VMEM((27, 32, 256), BF)],
        compiler_params=LARGE,
        name="early",
    )(x, c, *pin(*cols, weights[0]), w_down, *pin(*weights[2:]))


def level(rows, inner, weights, w_down):
    w_fwd, w_bwd, w_up, w_even, w_odd = weights
    return pl.pallas_call(
        level_kernel,
        out_shape=(
            held((4, 640, 128)),
            held((4, 640, 128)),
            held((8, 32, 384)),
            held((2, 32, 256)),
            held((7, 32, 512)),
        ),
        scratch_shapes=[
            pltpu.VMEM((1160, 128), F32),
            pltpu.VMEM((2, 1160, 128), F32),
            pltpu.VMEM((1032, 128), F32),
            pltpu.VMEM((7, 72, 128), F32),
            pltpu.VMEM((4, 72, 128), F32),
            pltpu.VMEM((8, 32, 512), BF),
            pltpu.VMEM((2, 32, 512), BF),
            pltpu.VMEM((8, 32, 256), F32),
            pltpu.VMEM((4, 32, 512), BF),
            pltpu.VMEM((2, 32, 256), BF),
            pltpu.VMEM((5, 32, 256), BF),
        ],
        compiler_params=LARGE,
        name="level",
    )(*pin(*rows, *inner[:5], *inner[7:], w_fwd), w_down, *pin(w_up, w_even, w_odd))


def late(*args):
    return pl.pallas_call(
        late_kernel,
        out_shape=(jax.ShapeDtypeStruct((32, 56, 128), BF),) * 2,
        scratch_shapes=[pltpu.VMEM((32, 72, 128), F32)],
        compiler_params=SMALL,
        name="late",
    )(*pin(*args))


def pairs(axis):
    count = lax.axis_size(axis)
    both = []
    for first in (0, 1):
        swaps = [(i, i + 1) for i in range(first, count - 1, 2)]
        both.append(swaps + [(b, a) for a, b in swaps])
    return both


def swap(longer, shorter, axis):
    even, odd = pairs(axis)
    return lax.ppermute(longer, axis, odd), lax.ppermute(shorter, axis, even)


def store_pair(odd, forward, backward, even_first, odd_first):
    even_first[...] = jnp.where(odd, backward, forward).astype(BF)
    odd_first[...] = jnp.where(odd, forward, backward).astype(BF)


def cols_kernel(x_last, x_first, c_last, c_first, col_b, col_a):
    rightward = jnp.concatenate([x_last[:, 4:8], c_last[:, 4:8]], axis=0).astype(F32)
    leftward = jnp.concatenate([x_first[:, 0:4], c_first[:, 0:4]], axis=0).astype(F32)
    store_pair(lax.axis_index("col") % 2 == 1, rightward, leftward, col_a, col_b)


def rows_kernel(x_last, x_first, c_last, c_first, col_b, col_a, row_b, row_a):
    left, right = swapped(lax.axis_index("col") % 2 == 1, col_b, col_a)

    def side(x, c, x_rows, c_rows):
        own = jnp.concatenate([x[...], c[...]], axis=0).astype(F32)
        after = jnp.concatenate([right[x_rows], right[c_rows]], axis=0)
        before = jnp.concatenate([left[x_rows], left[c_rows]], axis=0)
        return jnp.concatenate([own, after, before], axis=1)

    down = side(x_last, c_last, slice(28, 32), slice(62, 64))
    up = side(x_first, c_first, slice(0, 4), slice(32, 34))
    store_pair(lax.axis_index("row") % 2 == 1, down, up, row_a, row_b)


def row_block(count, at):
    return pl.BlockSpec((count, 56, 128), lambda i: (at, 0, 0))


def col_block(at):
    return pl.BlockSpec((32, 8, 128), lambda i: (0, at, 0))


def column_halo(x, c):
    whole = pl.BlockSpec((64, 4, 128), lambda i: (0, 0, 0))
    first, second = pl.pallas_call(
        cols_kernel,
        grid=(1,),
        out_shape=(jax.ShapeDtypeStruct((64, 4, 128), BF),) * 2,
        in_specs=[col_block(at) for at in (6, 0, 6, 0)],
        out_specs=(whole, whole),
        compiler_params=SMALL,
        name="cols",
    )(*far(x, x, c, c))
    return swap(first, second, "col")


def row_halo(x, c, cols):
    whole = pl.BlockSpec((6, 64, 128), lambda i: (0, 0, 0))
    first, second = pl.pallas_call(
        rows_kernel,
        grid=(1,),
        out_shape=(jax.ShapeDtypeStruct((6, 64, 128), BF),) * 2,
        in_specs=[row_block(4, 7), row_block(4, 0), row_block(2, 15), row_block(2, 0)]
        + [pl.BlockSpec((64, 4, 128), lambda i: (0, 0, 0))] * 2,
        out_specs=(whole, whole),
        compiler_params=SMALL,
        name="rows",
    )(x, x, c, c, *pin(*cols))
    return swap(first, second, "row")


def local_terms(inputs, cotangent, w_conv, w_down, w_up):
    flat_down = w_down.reshape(1152, 256)
    weights = prepare_weights(w_conv, w_down, w_up)
    cols = column_halo(inputs, cotangent)
    rows = row_halo(inputs, cotangent, cols)
    inner = early(inputs, cotangent, cols, weights, flat_down)
    keep, send, f3_rim, coarse_rim, g4_rim = level(rows, inner, weights, flat_down)
    held_back = (inner[2], f3_rim, inner[6], coarse_rim, inner[5], g4_rim, weights[2], weights[1])
    return keep, send, held_back


def spread_kernel(received, out, total, stage):
    total[...] = jnp.sum(received[...].astype(F32), axis=0)
    for k in range(20):
        first = (k // 10) * 320 + k % 10
        stage[pl.ds(first, 32, stride=10), :] = total[32 * k : 32 * k + 32, :]
    out[...] = stage[0:640, :].astype(BF)


def finish_kernel(scale, received, conv, down, up, stage):
    total = received[0:80, :].astype(F32)
    for chunk in range(1, 8):
        total = total + received[80 * chunk : 80 * chunk + 80, :].astype(F32)
    stage[...] = total
    rows = stage[0:10, :]
    for holder in range(1, 8):
        rows = rows + stage[10 * holder : 10 * holder + 10, :]
    rows = rows * scale
    for which in range(4):

        @pl.when(lax.axis_index("col") % 4 == which)
        def _():
            for ref, base, names, size in (
                (conv, 0, CONV_ROWS, 288), (down, 3, DOWN_ROWS, 576), (up, 8, UP_ROWS, 256)
            ):
                start = (base - names[which][0]) * 128 + which * size
                done = 0
                while done < size:
                    row, lane = divmod(start + done, 128)
                    count = min(128 - lane, size - done)
                    ref[pl.ds(done, count)] = rows[row, lane : lane + count]
                    done += count


def coordinates():
    def device(x, y, z, core):
        return (x * 4 + z // 2) * 32 + (z % 2) * 16 + y * 2 + core

    across = [
        [device(x, y, z, k) for x in range(4)]
        for z in range(8) for y in range(8) for k in range(2)
    ]
    plane = [
        [device(x, 2 * y + low, z, k) for low in range(2) for z in range(8) for y in range(4)]
        for x in range(4) for k in range(2)
    ]
    return across, plane


def reduce_owners(keep, send, scale, rest):
    mesh = ("row", "col")
    across, plane = coordinates()
    other = lax.ppermute(send, "col", [(i, i ^ 1) for i in range(32)])
    pair = (keep.astype(F32) + other.astype(F32)).astype(BF)
    got = lax.all_to_all(pair, mesh, 0, 0, axis_index_groups=across, tiled=True)
    spread = pl.pallas_call(
        spread_kernel,
        out_shape=jax.ShapeDtypeStruct((640, 128), BF),
        scratch_shapes=[pltpu.VMEM((640, 128), F32), pltpu.VMEM((656, 128), F32)],
        compiler_params=SMALL,
        name="spread",
    )(*pin(got))
    rim, _ = lax.optimization_barrier((rest[5], spread))
    rest = (*rest[:5], rim, *rest[6:])
    spread = spread.reshape(64, 5, 2, 128)
    got = lax.all_to_all(spread, mesh, 0, 0, axis_index_groups=plane, tiled=True)
    got = got.reshape(640, 128)
    sums = pl.pallas_call(
        functools.partial(finish_kernel, scale),
        out_shape=tuple(jax.ShapeDtypeStruct((n,), F32) for n in (288, 576, 256)),
        scratch_shapes=[pltpu.VMEM((80, 128), F32)],
        compiler_params=SMALL,
        name="finish",
    )(*pin(got))
    return (*late(*rest), *sums)


def body(inputs, cotangent, w_conv, w_down, w_up):
    keep, send, rest = local_terms(inputs, cotangent, w_conv, w_down, w_up)
    rows, cols, _ = inputs.shape
    scale = 1.0 / math.sqrt(rows * lax.axis_size("row") * cols * lax.axis_size("col"))
    return reduce_owners(keep, send, scale, rest)


def solution(mesh):
    grid = P("row", "col", None)
    flat = P(("row", "col"))
    return jax.shard_map(
        body,
        mesh=mesh,
        in_specs=(grid, grid, P(), P(), P()),
        out_specs=(grid, grid, flat, flat, flat),
        check_vma=False,
    )
```

```python
import functools
import math

import jax
import jax.numpy as jnp
from jax import lax
from jax.experimental import pallas as pl
from jax.experimental.pallas import tpu as pltpu
from jax.sharding import PartitionSpec as P

BF = jnp.bfloat16
F32 = jnp.float32
NN = (((1,), (0,)), ((), ()))
NT = (((1,), (1,)), ((), ()))
TN = (((0,), (0,)), ((), ()))
SMALL = pltpu.CompilerParams(vmem_limit_bytes=8 * 1024 * 1024)


def held(shape, dtype=BF):
    return pltpu.VMEM(shape, dtype)


def far(*arrays):
    return tuple(pltpu.with_memory_space_constraint(a, pltpu.HBM) for a in arrays)


def pin(*arrays):
    return tuple(pltpu.with_memory_space_constraint(a, pltpu.VMEM) for a in arrays)


def swapped(odd, one, two):
    one, two = one[...].astype(F32), two[...].astype(F32)
    return jnp.where(odd, two, one), jnp.where(odd, one, two)


def mm(left, right, dims):
    return lax.dot_general(left, right, dims, preferred_element_type=F32)


def sigmoid(value):
    return 1.0 / (1.0 + jnp.exp(-value))


def weights_kernel(wc, wd, wu, conv_fwd, conv_bwd, up, down_even, down_odd):
    zero = jnp.zeros((128, 128), BF)
    for p in range(3):
        for blk in range(4):
            rows = slice(blk * 128, (blk + 1) * 128)
            conv_fwd[p, rows, 0:128] = wc[p, blk] if blk < 3 else zero
            conv_fwd[p, rows, 128:256] = wc[p, blk - 1] if blk > 0 else zero
            conv_bwd[p, 0:128, rows] = wc[p, 2 - blk] if blk < 3 else zero
            conv_bwd[p, 128:256, rows] = wc[p, 3 - blk] if blk > 0 else zero
    for p in range(2):
        for q in range(2):
            up[:, (2 * p + q) * 128 : (2 * p + q + 1) * 128] = wu[p, q]
    wide = jnp.zeros((128, 256), BF)
    down_even[0:128, 0:256] = wd[1, 1]
    down_even[0:128, 256:512] = wide
    down_even[128:256, 0:256] = wd[1, 2]
    down_even[128:256, 256:512] = wd[1, 0]
    down_odd[0:128, 0:256] = wd[2, 1]
    down_odd[0:128, 256:512] = wide
    down_odd[0:128, 512:768] = wd[0, 1]
    down_odd[0:128, 768:1024] = wide
    down_odd[128:256, 0:256] = wd[2, 2]
    down_odd[128:256, 256:512] = wd[2, 0]
    down_odd[128:256, 512:768] = wd[0, 2]
    down_odd[128:256, 768:1024] = wd[0, 0]


def prepare_weights(w_conv, w_down, w_up):
    shapes = ((3, 512, 256), (3, 256, 512), (256, 512), (256, 512), (256, 1024))
    return pl.pallas_call(
        weights_kernel,
        out_shape=tuple(held(s) for s in shapes),
        compiler_params=SMALL,
        name="weights",
    )(w_conv, w_down, w_up)


CONV_ROWS = ((0, 1, 2), (2, 3, 4), (4, 5, 6), (6, 7, 8))
DOWN_ROWS = ((0, 1, 2, 3, 4), (4, 5, 6, 7, 8), (9, 10, 11, 12, 13), (13, 14, 15, 16, 17))
UP_ROWS = ((0, 1), (2, 3), (4, 5), (6, 7))


def pack(core, ref, conv_acc, down_acc, up_acc):
    k = 0
    for owner in (core, core + 2):
        for row in CONV_ROWS[owner]:
            value = conv_acc[pl.ds(row, 128, stride=9), :]
            ref[:, 32 * k : 32 * k + 32, :] = value.reshape(4, 32, 128).astype(BF)
            k += 1
        for row in DOWN_ROWS[owner]:
            value = down_acc[row % 2, pl.ds(row // 2, 128, stride=9), :]
            ref[:, 32 * k : 32 * k + 32, :] = value.reshape(4, 32, 128).astype(BF)
            k += 1
        for row in UP_ROWS[owner]:
            value = up_acc[pl.ds(row, 128, stride=8), :]
            ref[:, 32 * k : 32 * k + 32, :] = value.reshape(4, 32, 128).astype(BF)
            k += 1


def rows_at(parts, indices):
    found = []
    for index in indices:
        for first, count, ref, place in parts:
            if first <= index < first + count:
                found.append(ref[place + index - first])
                break
    return jnp.concatenate(found, axis=0)


def x4_parts(inner, rim):
    return ((0, 4, rim, 0), (4, 32, inner, 0), (36, 4, rim, 4))


def c4_parts(inner, rim):
    return ((0, 1, rim, 0), (1, 16, inner, 0), (17, 1, rim, 1))


def f3_parts(inner, rim):
    return ((0, 4, rim, 0), (4, 30, inner, 0), (34, 4, rim, 4))


def gs_parts(inner, rim):
    return ((0, 2, rim, 0), (2, 14, inner, 0), (16, 2, rim, 2))


def own_parts(inner, rim):
    return ((0, 1, rim, 0), (1, 14, inner, 0), (15, 1, rim, 1))


def column_masks():
    at_col = lax.axis_index("col")
    half = lax.broadcasted_iota(jnp.int32, (32, 256), 0) - 2
    own = (half >= 0) & (half < 28)
    last = lax.axis_size("col") - 1
    in_grid = ((half >= 0) | (at_col != 0)) & ((half < 28) | (at_col != last))
    return jnp.where(in_grid, 1.0, 0.0), jnp.where(own, 1.0, 0.0)


def row_masks():
    at_row = lax.axis_index("row")
    last = lax.axis_size("row") - 1
    return jnp.where(at_row == 0, 0.0, 1.0), jnp.where(at_row == last, 0.0, 1.0)


def per_row(value, mask):
    count = value.shape[0] // 32
    return (value.reshape(count, 32, 256) * mask[None]).reshape(count * 32, 256)


def clear_sides(ref):
    ref[:, 0:8, :] = jnp.zeros((ref.shape[0], 8, 128), F32)
    ref[:, 64:72, :] = jnp.zeros((ref.shape[0], 8, 128), F32)


def split_x(xs, x4, places):
    for r, place in enumerate(places):
        for k in range(4):
            x4[place, :, k * 128 : (k + 1) * 128] = xs[r, pl.ds(3 + k, 32, stride=2), :].astype(BF)


def split_c(cs, c4):
    for ai in range(c4.shape[0]):
        for p in range(2):
            for q in range(2):
                k = 2 * p + q
                c4[ai, :, k * 128 : (k + 1) * 128] = cs[
                    2 * ai + p, pl.ds(4 + q, 32, stride=2), :
                ].astype(BF)


def fine_rows(x4, indices, w_fwd, in_grid):
    pre = None
    for p in range(3):
        term = mm(rows_at(x4, [i + p for i in indices]), w_fwd[p], NN)
        pre = term if pre is None else pre + term
    sig = sigmoid(pre)
    return per_row(pre * sig, in_grid), sig * (1.0 + pre * (1.0 - sig))


def store_fine(fine, slopes, f3, slope, first, count):
    behind = pltpu.roll(fine[:, 128:256], 1, 0).astype(BF).reshape(count, 32, 128)
    f3[first : first + count, :, 0:128] = behind
    f3[first : first + count, :, 128:384] = fine.astype(BF).reshape(count, 32, 256)
    slope[first : first + count] = slopes.reshape(count, 32, 256)


def coarse_rows(f3, c4, ais, w_down, w_up):
    parts = [rows_at(f3, [2 * ai + p for ai in ais]) for p in range(3)]
    cpre = mm(jnp.concatenate(parts, axis=1), w_down[...], NN)
    sig = sigmoid(cpre)
    grad = mm(rows_at(c4, ais), w_up[...], NT) * (sig * (1.0 + cpre * (1.0 - sig)))
    return cpre * sig, grad


def store_coarse(grad, gs, first, count):
    ahead = pltpu.roll(grad, count * 32 - 1, 0)
    gs[first : first + count, :, 0:256] = grad.astype(BF).reshape(count, 32, 256)
    gs[first : first + count, :, 256:512] = ahead.astype(BF).reshape(count, 32, 256)


def grad_rows(gs, c4, slope, ais, odd, w_even, w_odd, in_grid):
    nexts = [ai + 1 for ai in ais]
    below = rows_at(gs, nexts)
    if odd:
        spread = mm(jnp.concatenate([rows_at(gs, ais), below], axis=1), w_odd[...], NT)
        cot = rows_at(c4, ais)[:, 256:512]
    else:
        spread = mm(below, w_even[...], NT)
        cot = rows_at(c4, nexts)[:, 0:256]
    slopes = rows_at(slope, [2 * ai + (2 if odd else 3) for ai in ais])
    return per_row((cot.astype(F32) + spread) * slopes, in_grid)


def store_grad(grad, own, g4, pre_own, places, own_places):
    behind = pltpu.roll(grad[:, 128:256], 1, 0).astype(BF)
    ahead = pltpu.roll(grad[:, 0:128], grad.shape[0] - 1, 0).astype(BF)
    rounded = grad.astype(BF)
    kept = per_row(grad, own).astype(BF)
    for i, (place, own_place) in enumerate(zip(places, own_places)):
        rows = slice(i * 32, i * 32 + 32)
        g4[place, :, 0:128] = behind[rows]
        g4[place, :, 128:384] = rounded[rows]
        g4[place, :, 384:512] = ahead[rows]
        if own_place is not None:
            pre_own[own_place] = kept[rows]


def conv_taps(pre, x4, rows, p, flip):
    window = rows_at(x4, [i + p + 3 for i in rows])
    taps = []
    if flip:
        res = mm(window, pre, TN)
        for q in range(3):
            one, two = slice(q * 128, q * 128 + 128), slice(q * 128 + 128, q * 128 + 256)
            taps.append(res[one, 0:128] + res[two, 128:256])
    else:
        res = mm(pre, window, TN)
        for q in range(3):
            one, two = slice(q * 128, q * 128 + 128), slice(q * 128 + 128, q * 128 + 256)
            taps.append((res[0:128, one] + res[128:256, two]).T)
    return taps


def g4_parts(inner, rim):
    return ((0, 3, rim, 0), (3, 27, inner, 0), (30, 4, rim, 3))


def early_kernel(
    x, c, col_b, col_a, w_fwd, w_down, w_up, w_even, w_odd,
    x4, c4, f3, slope, gs, g4, coarse_own, conv_part, up_part, down_part,
    xs, cs, g_own, pre_own,
):
    left, right = swapped(lax.axis_index("col") % 2 == 1, col_b, col_a)
    for ref, own_block, first in ((xs, x, 0), (cs, c, 32)):
        clear_sides(ref)
        ref[:, 8:64, :] = own_block[...].astype(F32)
        ref[:, 4:8, :] = left[first : first + 32]
        ref[:, 64:68, :] = right[first : first + 32]
    split_x(xs, x4, range(32))
    split_c(cs, c4)
    in_grid, own = column_masks()
    for first, count in ((4, 8), (12, 8), (20, 8), (28, 6)):
        fine, slopes = fine_rows(
            x4_parts(x4, None), range(first, first + count), w_fwd, in_grid
        )
        store_fine(fine, slopes, f3, slope, first - 4, count)
    for first in (2, 9):
        coarse, grad = coarse_rows(
            f3_parts(f3, None), c4_parts(c4, None), range(first, first + 7), w_down, w_up
        )
        store_coarse(grad, gs, first - 2, 7)
        coarse_own[first - 2 : first + 5] = per_row(coarse, own).astype(BF).reshape(7, 32, 256)
        g_own[first - 2 : first + 5] = per_row(grad, own).astype(BF).reshape(7, 32, 256)
    x4_all, c4_all, f3_all = x4_parts(x4, None), c4_parts(c4, None), f3_parts(f3, None)
    gs_all, slope_all = gs_parts(gs, None), f3_parts(slope, None)
    coarse_flat = coarse_own[...].reshape(448, 256)
    up_part[...] = mm(coarse_flat, rows_at(c4_all, range(2, 16)), TN)
    g_flat = g_own[...].reshape(448, 256)
    for p in range(3):
        window = rows_at(f3_all, [2 * a + p + 2 for a in range(1, 15)])
        down_part[p * 384 : (p + 1) * 384, :] = mm(window, g_flat, TN)
    for odd, ais in ((True, range(2, 9)), (True, range(9, 15)), (False, range(1, 8)), (False, range(8, 15))):
        grad = grad_rows(gs_all, c4_all, slope_all, ais, odd, w_even, w_odd, in_grid)
        at = [2 * ai - 3 + (0 if odd else 1) for ai in ais]
        store_grad(grad, own, g4, pre_own, at, at)
    flat = pre_own[...].reshape(864, 256)
    for p in range(3):
        for q, tap in enumerate(conv_taps(flat, x4_all, range(2, 29), p, False)):
            conv_part[(3 * p + q) * 128 : (3 * p + q + 1) * 128, :] = tap


def level_kernel(
    row_b, row_a, x4_in, c4_in, f3_in, slope_in, gs_in, conv_part, up_part, down_part,
    w_fwd, w_down, w_up, w_even, w_odd,
    keep, send, f3_rim, coarse_rim, g4_rim,
    conv_acc, down_acc, up_acc, xs, cs, x4_rim, c4_rim, slope_rim, gs_rim, g_rim, pre_rim,
):
    top, bot = swapped(lax.axis_index("row") % 2 == 1, row_b, row_a)
    for ref, at, value in (
        (xs, slice(0, 4), top[0:4]), (xs, slice(4, 7), bot[0:3]),
        (cs, slice(0, 2), top[4:6]), (cs, slice(2, 4), bot[4:6]),
    ):
        ref[at, 0:8, :] = jnp.zeros((value.shape[0], 8, 128), F32)
        ref[at, 64:72, :] = jnp.zeros((value.shape[0], 8, 128), F32)
        ref[at, 8:68, :] = value[:, 0:60]
        ref[at, 4:8, :] = value[:, 60:64]
    split_x(xs, x4_rim, range(7))
    x4_rim[7] = jnp.zeros((32, 512), BF)
    split_c(cs, c4_rim)
    in_grid, own = column_masks()
    keep_top, keep_bot = row_masks()
    x4, c4 = x4_parts(x4_in, x4_rim), c4_parts(c4_in, c4_rim)
    f3, slope = f3_parts(f3_in, f3_rim), f3_parts(slope_in, slope_rim)
    gs = gs_parts(gs_in, gs_rim)

    fine, slopes = fine_rows(x4, (0, 1, 2, 3, 34, 35, 36, 37), w_fwd, in_grid)
    fine = jnp.concatenate(
        [fine[0:96] * keep_top, fine[96:160], fine[160:256] * keep_bot], axis=0
    )
    store_fine(fine, slopes, f3_rim, slope_rim, 0, 8)

    coarse, grad = coarse_rows(f3, c4, (0, 1, 16, 17), w_down, w_up)
    store_coarse(grad, gs_rim, 0, 4)
    coarse_rim[...] = per_row(coarse[32:96], own).astype(BF).reshape(2, 32, 256)
    g_rim[...] = per_row(grad[32:96], own).astype(BF).reshape(2, 32, 256)

    res = up_part[...] + mm(coarse_rim[...].reshape(64, 256), rows_at(c4, (1, 16)), TN)
    for k in range(4):
        up_acc[k * 256 : (k + 1) * 256, :] = res[:, k * 128 : (k + 1) * 128]
    g_flat = g_rim[...].reshape(64, 256)
    for p in range(3):
        at = slice(p * 384, (p + 1) * 384)
        res = down_part[at, :] + mm(rows_at(f3, (p + 2, p + 32)), g_flat, TN)
        for side in range(2):
            down_acc[side, at, :] = res[:, side * 128 : (side + 1) * 128]

    grad = grad_rows(gs, c4, slope, (0, 1, 15, 16), True, w_even, w_odd, in_grid)
    grad = jnp.concatenate([grad[0:32] * keep_top, grad[32:]], axis=0)
    store_grad(grad, own, g4_rim, pre_rim, (0, 2, 3, 5), (None, 1, 2, 4))
    grad = grad_rows(gs, c4, slope, (0, 15, 16), False, w_even, w_odd, in_grid)
    grad = jnp.concatenate([grad[0:64], grad[64:] * keep_bot], axis=0)
    store_grad(grad, own, g4_rim, pre_rim, (1, 4, 6), (0, 3, None))

    flat = pre_rim[...].reshape(160, 256)
    for p in range(3):
        for q, tap in enumerate(conv_taps(flat, x4, (0, 1, 29, 30, 31), p, True)):
            at = slice((3 * p + q) * 128, (3 * p + q + 1) * 128)
            conv_acc[at, :] = conv_part[at, :] + tap

    odd_col = lax.axis_index("col") % 2 == 1

    @pl.when(jnp.logical_not(odd_col))
    def _():
        pack(0, keep, conv_acc, down_acc, up_acc)
        pack(1, send, conv_acc, down_acc, up_acc)

    @pl.when(odd_col)
    def _():
        pack(1, keep, conv_acc, down_acc, up_acc)
        pack(0, send, conv_acc, down_acc, up_acc)


def late_kernel(
    f3_in, f3_rim, coarse_in, coarse_rim, g4_in, g4_rim, w_up, w_bwd, out, gx, mix
):
    g4 = g4_parts(g4_in, g4_rim)
    f3 = f3_parts(f3_in, f3_rim)
    coarse = own_parts(coarse_in, coarse_rim)
    for first in (0, 8):
        up = mm(rows_at(coarse, range(first, first + 8)), w_up[...], NN)
        for a in range(first, first + 8):
            for p in range(2):
                for q in range(2):
                    k = 2 * p + q
                    value = up[(a - first) * 32 : (a - first + 1) * 32, k * 128 : (k + 1) * 128]
                    fine = rows_at(f3, [2 * a + p + 3])[:, 128 + q * 128 : 256 + q * 128]
                    value = value + fine.astype(F32)
                    mix[2 * a + p, pl.ds(4 + q, 32, stride=2), :] = value
    out[...] = mix[:, 8:64, :].astype(BF)
    for first in (0, 8, 16, 24):
        total = None
        for p in range(3):
            window = rows_at(g4, range(first + 2 - p, first + 10 - p))
            term = mm(window, w_bwd[p], NT)
            total = term if total is None else total + term
        for i in range(first, first + 8):
            for q in range(2):
                mix[i, pl.ds(4 + q, 32, stride=2), :] = total[
                    (i - first) * 32 : (i - first + 1) * 32, q * 128 : (q + 1) * 128
                ]
    gx[...] = mix[:, 8:64, :].astype(BF)


LARGE = pltpu.CompilerParams(vmem_limit_bytes=16 * 1024 * 1024)


def early(x, c, cols, weights, w_down):
    return pl.pallas_call(
        early_kernel,
        out_shape=(
            held((32, 32, 512)),
            held((16, 32, 512)),
            held((30, 32, 384)),
            held((30, 32, 256), F32),
            held((14, 32, 512)),
            held((27, 32, 512)),
            held((14, 32, 256)),
            held((1152, 128), F32),
            held((256, 512), F32),
            held((1152, 256), F32),
        ),
        scratch_shapes=[pltpu.VMEM((32, 72, 128), F32)] * 2
        + [pltpu.VMEM((14, 32, 256), BF), pltpu.VMEM((27, 32, 256), BF)],
        compiler_params=LARGE,
        name="early",
    )(x, c, *pin(*cols, weights[0]), w_down, *pin(*weights[2:]))


def level(rows, inner, weights, w_down):
    w_fwd, w_bwd, w_up, w_even, w_odd = weights
    return pl.pallas_call(
        level_kernel,
        out_shape=(
            held((4, 640, 128)),
            held((4, 640, 128)),
            held((8, 32, 384)),
            held((2, 32, 256)),
            held((7, 32, 512)),
        ),
        scratch_shapes=[
            pltpu.VMEM((1160, 128), F32),
            pltpu.VMEM((2, 1160, 128), F32),
            pltpu.VMEM((1032, 128), F32),
            pltpu.VMEM((7, 72, 128), F32),
            pltpu.VMEM((4, 72, 128), F32),
            pltpu.VMEM((8, 32, 512), BF),
            pltpu.VMEM((2, 32, 512), BF),
            pltpu.VMEM((8, 32, 256), F32),
            pltpu.VMEM((4, 32, 512), BF),
            pltpu.VMEM((2, 32, 256), BF),
            pltpu.VMEM((5, 32, 256), BF),
        ],
        compiler_params=LARGE,
        name="level",
    )(*pin(*rows, *inner[:5], *inner[7:], w_fwd), w_down, *pin(w_up, w_even, w_odd))


def late(*args):
    return pl.pallas_call(
        late_kernel,
        out_shape=(jax.ShapeDtypeStruct((32, 56, 128), BF),) * 2,
        scratch_shapes=[pltpu.VMEM((32, 72, 128), F32)],
        compiler_params=SMALL,
        name="late",
    )(*pin(*args))


def pairs(axis):
    count = lax.axis_size(axis)
    both = []
    for first in (0, 1):
        swaps = [(i, i + 1) for i in range(first, count - 1, 2)]
        both.append(swaps + [(b, a) for a, b in swaps])
    return both


def swap(longer, shorter, axis):
    even, odd = pairs(axis)
    return lax.ppermute(longer, axis, odd), lax.ppermute(shorter, axis, even)


def store_pair(odd, forward, backward, even_first, odd_first):
    even_first[...] = jnp.where(odd, backward, forward).astype(BF)
    odd_first[...] = jnp.where(odd, forward, backward).astype(BF)


def cols_kernel(x_last, x_first, c_last, c_first, col_b, col_a):
    rightward = jnp.concatenate([x_last[:, 4:8], c_last[:, 4:8]], axis=0).astype(F32)
    leftward = jnp.concatenate([x_first[:, 0:4], c_first[:, 0:4]], axis=0).astype(F32)
    store_pair(lax.axis_index("col") % 2 == 1, rightward, leftward, col_a, col_b)


def rows_kernel(x_last, x_first, c_last, c_first, col_b, col_a, row_b, row_a):
    left, right = swapped(lax.axis_index("col") % 2 == 1, col_b, col_a)

    def side(x, c, x_rows, c_rows):
        own = jnp.concatenate([x[...], c[...]], axis=0).astype(F32)
        after = jnp.concatenate([right[x_rows], right[c_rows]], axis=0)
        before = jnp.concatenate([left[x_rows], left[c_rows]], axis=0)
        return jnp.concatenate([own, after, before], axis=1)

    down = side(x_last, c_last, slice(28, 32), slice(62, 64))
    up = side(x_first, c_first, slice(0, 4), slice(32, 34))
    store_pair(lax.axis_index("row") % 2 == 1, down, up, row_a, row_b)


def row_block(count, at):
    return pl.BlockSpec((count, 56, 128), lambda i: (at, 0, 0))


def col_block(at):
    return pl.BlockSpec((32, 8, 128), lambda i: (0, at, 0))


def column_halo(x, c):
    whole = pl.BlockSpec((64, 4, 128), lambda i: (0, 0, 0))
    first, second = pl.pallas_call(
        cols_kernel,
        grid=(1,),
        out_shape=(jax.ShapeDtypeStruct((64, 4, 128), BF),) * 2,
        in_specs=[col_block(at) for at in (6, 0, 6, 0)],
        out_specs=(whole, whole),
        compiler_params=SMALL,
        name="cols",
    )(*far(x, x, c, c))
    return swap(first, second, "col")


def row_halo(x, c, cols):
    whole = pl.BlockSpec((6, 64, 128), lambda i: (0, 0, 0))
    first, second = pl.pallas_call(
        rows_kernel,
        grid=(1,),
        out_shape=(jax.ShapeDtypeStruct((6, 64, 128), BF),) * 2,
        in_specs=[row_block(4, 7), row_block(4, 0), row_block(2, 15), row_block(2, 0)]
        + [pl.BlockSpec((64, 4, 128), lambda i: (0, 0, 0))] * 2,
        out_specs=(whole, whole),
        compiler_params=SMALL,
        name="rows",
    )(x, x, c, c, *pin(*cols))
    return swap(first, second, "row")


def local_terms(inputs, cotangent, w_conv, w_down, w_up):
    flat_down = w_down.reshape(1152, 256)
    weights = prepare_weights(w_conv, w_down, w_up)
    cols = column_halo(inputs, cotangent)
    weights, cols = lax.optimization_barrier((weights, cols))
    rows = row_halo(inputs, cotangent, cols)
    inner = early(inputs, cotangent, cols, weights, flat_down)
    keep, send, f3_rim, coarse_rim, g4_rim = level(rows, inner, weights, flat_down)
    held_back = (inner[2], f3_rim, inner[6], coarse_rim, inner[5], g4_rim, weights[2], weights[1])
    return keep, send, held_back


def spread_kernel(received, out, total, stage):
    total[...] = jnp.sum(received[...].astype(F32), axis=0)
    for k in range(20):
        first = (k // 10) * 320 + k % 10
        stage[pl.ds(first, 32, stride=10), :] = total[32 * k : 32 * k + 32, :]
    out[...] = stage[0:640, :].astype(BF)


def finish_kernel(scale, received, conv, down, up, stage):
    total = received[0:80, :].astype(F32)
    for chunk in range(1, 8):
        total = total + received[80 * chunk : 80 * chunk + 80, :].astype(F32)
    stage[...] = total
    rows = stage[0:10, :]
    for holder in range(1, 8):
        rows = rows + stage[10 * holder : 10 * holder + 10, :]
    rows = rows * scale
    for which in range(4):

        @pl.when(lax.axis_index("col") % 4 == which)
        def _():
            for ref, base, names, size in (
                (conv, 0, CONV_ROWS, 288), (down, 3, DOWN_ROWS, 576), (up, 8, UP_ROWS, 256)
            ):
                start = (base - names[which][0]) * 128 + which * size
                done = 0
                while done < size:
                    row, lane = divmod(start + done, 128)
                    count = min(128 - lane, size - done)
                    ref[pl.ds(done, count)] = rows[row, lane : lane + count]
                    done += count


def coordinates():
    def device(x, y, z, core):
        return (x * 4 + z // 2) * 32 + (z % 2) * 16 + y * 2 + core

    across = [
        [device(x, y, z, k) for x in range(4)]
        for z in range(8) for y in range(8) for k in range(2)
    ]
    plane = [
        [device(x, 2 * y + low, z, k) for low in range(2) for z in range(8) for y in range(4)]
        for x in range(4) for k in range(2)
    ]
    return across, plane


def reduce_owners(keep, send, scale, rest):
    mesh = ("row", "col")
    across, plane = coordinates()
    other = lax.ppermute(send, "col", [(i, i ^ 1) for i in range(32)])
    pair = (keep.astype(F32) + other.astype(F32)).astype(BF)
    got = lax.all_to_all(pair, mesh, 0, 0, axis_index_groups=across, tiled=True)
    spread = pl.pallas_call(
        spread_kernel,
        out_shape=jax.ShapeDtypeStruct((640, 128), BF),
        scratch_shapes=[pltpu.VMEM((640, 128), F32), pltpu.VMEM((656, 128), F32)],
        compiler_params=SMALL,
        name="spread",
    )(*pin(got))
    rim, _ = lax.optimization_barrier((rest[5], spread))
    rest = (*rest[:5], rim, *rest[6:])
    spread = spread.reshape(64, 5, 2, 128)
    got = lax.all_to_all(spread, mesh, 0, 0, axis_index_groups=plane, tiled=True)
    got = got.reshape(640, 128)
    sums = pl.pallas_call(
        functools.partial(finish_kernel, scale),
        out_shape=tuple(jax.ShapeDtypeStruct((n,), F32) for n in (288, 576, 256)),
        scratch_shapes=[pltpu.VMEM((80, 128), F32)],
        compiler_params=SMALL,
        name="finish",
    )(*pin(got))
    return (*late(*rest), *sums)


def body(inputs, cotangent, w_conv, w_down, w_up):
    keep, send, rest = local_terms(inputs, cotangent, w_conv, w_down, w_up)
    rows, cols, _ = inputs.shape
    scale = 1.0 / math.sqrt(rows * lax.axis_size("row") * cols * lax.axis_size("col"))
    return reduce_owners(keep, send, scale, rest)


def solution(mesh):
    grid = P("row", "col", None)
    flat = P(("row", "col"))
    return jax.shard_map(
        body,
        mesh=mesh,
        in_specs=(grid, grid, P(), P(), P()),
        out_specs=(grid, grid, flat, flat, flat),
        check_vma=False,
    )
```
